32 devices in a mesh: shard: 4 (over y, core), rep: 8 (over z, x).
Axes of the slice: x: 2, y: 2, z: 4, core: 2. Of those that a mesh axis runs over, the one named last changes fastest.
Arguments:
- tokens: bfloat16 [8, 512, 768], P('rep', 'shard'), may hold values from -6 to 6
- gain_one: bfloat16 [768], P('shard'), may hold values from 0.5 to 1.5
- qkv_weight: bfloat16 [768, 2304], P('shard'), may hold values from -6 to 6
- out_weight: bfloat16 [768, 768], P('shard'), may hold values from -2.5 to 2.5
- gain_two: bfloat16 [768], P('shard'), may hold values from 0.5 to 1.5
- in_weight: bfloat16 [768, 2304], P('shard'), may hold values from -0.21875 to 0.21875
- down_weight: bfloat16 [1152, 768], P('shard'), may hold values from -0.1875 to 0.1875
- grad_output: bfloat16 [8, 512, 768], P('rep', 'shard'), may hold values from -6 to 6
Outputs:
- output: bfloat16 [8, 512, 768], P('rep', 'shard')
- grad_tokens: float32 [8, 512, 768], P('rep', 'shard')
- grad_gain_one: float32 [768], P('shard')
- grad_qkv: float32 [768, 2304], P('shard')
- grad_out: float32 [768, 768], P('shard')
- grad_gain_two: float32 [768], P('shard')
- grad_in: float32 [768, 2304], P('shard')
- grad_down: float32 [1152, 768], P('shard')
The draws below stay inside these ranges and needn't reach their ends.
All inputs are finite; a program needn't handle non-finite values.
Results may differ from the reference program's by a relative error of at most 0.02.
Values may be sent and summed in bfloat16 or wider, within the bound.
A program may use at most 128 MiB of HBM per device.

```python
import jax
import jax.numpy as jnp
from jax import lax

D = 768
HEADS = 12
HEAD_DIM = 64
FF = 1152
TOK_DEV = 128
LEN = 512
SEQS = 8
N_SHARD = 4


def draw_qkv_weight(key, part):
    base = jnp.clip(jax.random.normal(key, (D, 3 * D), jnp.float32), -5.0, 5.0) * D ** (-0.5)
    return base.astype(jnp.bfloat16)


def block_levels(stream_key, dims, pieces, smallest, largest):
    level, own = 1.0, jax.random.fold_in(stream_key, 6)
    for dim, shards_of in pieces:
        heights = jnp.exp(jax.random.uniform(jax.random.fold_in(own, dim), (shards_of,), jnp.float32, smallest / len(pieces), largest / len(pieces)))
        level = level * jnp.repeat(heights, dims[dim] // shards_of).reshape([-1 if axis == dim else 1 for axis in range(len(dims))])
    return level


def scatter_about(rng, shape, deviation, bound, cuts=(), held_as=jnp.bfloat16):
    loudness = block_levels(rng, shape, cuts, -0.22, 0.18) if cuts else 1.0
    values = jax.random.normal(rng, shape, jnp.float32) * deviation * loudness
    return jnp.minimum(jnp.maximum(values, -bound), bound).astype(held_as)


def setup_inputs(seed: int = 0) -> dict:
    streams_of = jax.random.split(jax.random.key(seed), 9)
    return {
        "tokens": scatter_about(streams_of[0], (SEQS, LEN, D), 1.0, 6.0, ((0, 8), (1, 4))),
        "gain_one": jnp.clip(1.0 + 0.1 * jax.random.normal(streams_of[1], (D,), jnp.float32), 0.5, 1.5).astype(jnp.bfloat16),
        "qkv_weight": draw_qkv_weight(jax.random.fold_in(streams_of[8], 71), 0),
        "out_weight": scatter_about(streams_of[3], (D, D), (max(1, 4 * D // (TOK_DEV * N_SHARD))) ** -0.5, 2.5, ((0, 4),)),
        "gain_two": jnp.clip(1.0 + 0.1 * jax.random.normal(streams_of[4], (D,), jnp.float32), 0.5, 1.5).astype(jnp.bfloat16),
        "in_weight": scatter_about(streams_of[5], (D, 2 * FF), D ** -0.5, 0.21875, ((0, 4),)),
        "down_weight": scatter_about(streams_of[6], (FF, D), FF ** -0.5, 0.1875, ((0, 4),)),
        "grad_output": scatter_about(streams_of[7], (SEQS, LEN, D), 1.0, 6.0, ((0, 8), (1, 4))),
    }


EPSILON = 1e-05
THETA = 160000.0
SQRT_HALF = 0.7071067811865476
INV_SQRT_TAU = 0.3989422804014327

def layer_norm(values, gain):
    mean_row = lax.optimization_barrier(jnp.mean(values, axis=-1, keepdims=True))
    centred = values - mean_row
    variance = lax.optimization_barrier(jnp.mean(centred * centred, axis=-1, keepdims=True))
    inverse = lax.rsqrt(variance + EPSILON)
    normed = centred * inverse
    return (normed, inverse, normed * gain.astype(jnp.float32))

def norm_backward(grad_out, normed, inverse, gain):
    grad_normed = grad_out * gain.astype(jnp.float32)
    gain_grad = lax.optimization_barrier(jnp.sum(grad_out * normed, axis=0))
    first = lax.optimization_barrier(jnp.mean(grad_normed, axis=-1, keepdims=True))
    second = lax.optimization_barrier(jnp.mean(grad_normed * normed, axis=-1, keepdims=True))
    return (inverse * (grad_normed - first - normed * second), gain_grad)

def rotary_tables(positions, head_dim):
    half = head_dim // 2
    freq = THETA ** (-jnp.arange(half, dtype=jnp.float32) * 2.0 / head_dim)
    angles = positions.astype(jnp.float32)[:, None] * freq[None, :]
    angles = jnp.concatenate([angles, angles], axis=-1)
    return (jnp.cos(angles)[:, None, :], jnp.sin(angles)[:, None, :])

def rotate_half(values):
    half = values.shape[-1] // 2
    return jnp.concatenate([-values[..., half:], values[..., :half]], axis=-1)

def gelu_pair(inner):
    cdf = 0.5 * (1.0 + jax.scipy.special.erf(inner * SQRT_HALF))
    return (inner * cdf, cdf + inner * jnp.exp(-0.5 * inner * inner) * INV_SQRT_TAU)

def as_operand(values):
    return lax.optimization_barrier(values.astype(jnp.bfloat16)).astype(jnp.float32)

def sequence_pass(x_seq, grad_seq, gain_one, qkv_weight, out_weight, gain_two, in_weight, down_weight):
    length = x_seq.shape[0]
    scale = HEAD_DIM ** (-0.5)
    inputs = x_seq.astype(jnp.float32)
    normed_one, inverse_one, scaled_one = layer_norm(inputs, gain_one)
    hidden_one = scaled_one.astype(jnp.bfloat16)
    projected = jnp.dot(hidden_one, qkv_weight, preferred_element_type=jnp.float32)
    cosine, sine = rotary_tables(jnp.arange(length, dtype=jnp.int32), HEAD_DIM)
    queries = projected[:, :D].reshape(length, HEADS, HEAD_DIM)
    key_raw = projected[:, D:2 * D].reshape(length, HEADS, HEAD_DIM)
    query_rot = as_operand(queries * cosine + rotate_half(queries) * sine)
    key_rot = as_operand(key_raw * cosine + rotate_half(key_raw) * sine)
    value_rot = as_operand(projected[:, 2 * D:].reshape(length, HEADS, HEAD_DIM))
    scores = jnp.einsum('qhd,khd->hqk', query_rot, key_rot) * scale
    maxima = lax.optimization_barrier(jnp.max(scores, axis=-1))
    expo = jnp.exp(scores - maxima[..., None])
    totals = lax.optimization_barrier(jnp.sum(expo, axis=-1))
    accum = jnp.einsum('hqk,khd->hqd', as_operand(expo), value_rot)
    attended = (accum / totals[..., None]).transpose(1, 0, 2).reshape(length, D).astype(jnp.bfloat16)
    log_sum = maxima + jnp.log(totals)
    resid = inputs + jnp.dot(attended, out_weight, preferred_element_type=jnp.float32)
    normed_two, inverse_two, scaled_two = layer_norm(resid, gain_two)
    hidden_two = scaled_two.astype(jnp.bfloat16)
    upper = jnp.dot(hidden_two, in_weight, preferred_element_type=jnp.float32)
    inner = upper[:, :FF]
    gate_half = upper[:, FF:]
    gelu_value, gelu_slope = gelu_pair(inner)
    act = (gelu_value * gate_half).astype(jnp.bfloat16)
    output = (resid + jnp.dot(act, down_weight, preferred_element_type=jnp.float32)).astype(jnp.bfloat16)
    grad_b = grad_seq
    grad_f = grad_seq.astype(jnp.float32)
    grad_down = jnp.dot(act.T, grad_b, preferred_element_type=jnp.float32)
    grad_act = jnp.dot(grad_b, down_weight.T, preferred_element_type=jnp.float32)
    grad_upper = jnp.concatenate([grad_act * gate_half * gelu_slope, grad_act * gelu_value], axis=-1).astype(jnp.bfloat16)
    grad_in = jnp.dot(hidden_two.T, grad_upper, preferred_element_type=jnp.float32)
    grad_h2 = jnp.dot(grad_upper, in_weight.T, preferred_element_type=jnp.float32)
    norm_grad_two, grad_gain_two = norm_backward(grad_h2, normed_two, inverse_two, gain_two)
    grad_resid = grad_f + norm_grad_two
    resid_b = grad_resid.astype(jnp.bfloat16)
    grad_out = jnp.dot(attended.T, resid_b, preferred_element_type=jnp.float32)
    grad_att = jnp.dot(resid_b, out_weight.T, preferred_element_type=jnp.float32).astype(jnp.bfloat16)
    grad_heads = grad_att.astype(jnp.float32).reshape(length, HEADS, HEAD_DIM)
    att_heads = attended.astype(jnp.float32).reshape(length, HEADS, HEAD_DIM)
    delta = lax.optimization_barrier(jnp.sum(grad_heads * att_heads, axis=-1)).T
    probs = jnp.exp(scores - log_sum[..., None])
    grad_value = jnp.einsum('hqk,qhd->khd', as_operand(probs), grad_heads)
    grad_probs = jnp.einsum('qhd,khd->hqk', grad_heads, value_rot)
    grad_scores = as_operand(probs * (grad_probs - delta[..., None]) * scale)
    grad_qr = jnp.einsum('hqk,khd->qhd', grad_scores, key_rot)
    grad_kr = jnp.einsum('hqk,qhd->khd', grad_scores, query_rot)
    grad_q = grad_qr * cosine - rotate_half(grad_qr) * sine
    grad_k = grad_kr * cosine - rotate_half(grad_kr) * sine
    grad_projected = jnp.concatenate([grad_q.reshape(length, D), grad_k.reshape(length, D), grad_value.reshape(length, D)], axis=-1).astype(jnp.bfloat16)
    grad_qkv = jnp.dot(hidden_one.T, grad_projected, preferred_element_type=jnp.float32)
    grad_h1 = jnp.dot(grad_projected, qkv_weight.T, preferred_element_type=jnp.float32)
    norm_grad_one, grad_gain_one = norm_backward(grad_h1, normed_one, inverse_one, gain_one)
    grad_tokens = grad_resid + norm_grad_one
    return (output, grad_tokens, (grad_gain_one, grad_qkv, grad_out, grad_gain_two, grad_in, grad_down))

def reference(tokens, gain_one, qkv_weight, out_weight, gain_two, in_weight, down_weight, grad_output):

    def step(carry, pair):
        output, grad_tokens, grads = sequence_pass(pair[0], pair[1], gain_one, qkv_weight, out_weight, gain_two, in_weight, down_weight)
        carry = tuple((total + part for total, part in zip(carry, grads)))
        return (carry, (output, grad_tokens))
    start = (jnp.zeros((D,), jnp.float32), jnp.zeros((D, 3 * D), jnp.float32), jnp.zeros((D, D), jnp.float32), jnp.zeros((D,), jnp.float32), jnp.zeros((D, 2 * FF), jnp.float32), jnp.zeros((FF, D), jnp.float32))
    sums, stacked = lax.scan(step, start, (tokens, grad_output))
    return (stacked[0], stacked[1], sums[0], sums[1], sums[2], sums[3], sums[4], sums[5])
```

```python
import functools

import jax
import jax.numpy as jnp
import numpy as np
from jax import lax
from jax.experimental import pallas as pl
from jax.experimental.pallas import tpu as pltpu
from jax.sharding import PartitionSpec as P

HEAD_DIM = 64
EPSILON = 1e-05
THETA = 160000.0
SQRT_HALF = 0.7071067811865476
INV_SQRT_TAU = 0.3989422804014327
MESH_ID = pl.DeviceIdType.MESH
LANES = 128
VMEM = pl.BlockSpec(memory_space=pltpu.VMEM)
F32 = jnp.float32
B16 = jnp.bfloat16
SEMAPHORES = 448


def normalize(values):
    mean_row = jnp.mean(values, axis=-1, keepdims=True)
    centred = values - mean_row
    variance = jnp.mean(centred * centred, axis=-1, keepdims=True)
    inverse = lax.rsqrt(variance + EPSILON)
    return (centred * inverse, inverse)


def norm_backward(grad_out, normed, inverse, gain):
    grad_normed = grad_out * gain
    gain_grad = jnp.sum(grad_out * normed, axis=0, keepdims=True)
    first = jnp.mean(grad_normed, axis=-1, keepdims=True)
    second = jnp.mean(grad_normed * normed, axis=-1, keepdims=True)
    return (inverse * (grad_normed - first - normed * second), gain_grad)


def gelu_pair(inner):
    cdf = 0.5 * (1.0 + lax.erf(inner * SQRT_HALF))
    return (inner * cdf, cdf + inner * jnp.exp(-0.5 * inner * inner) * INV_SQRT_TAU)


def dot(left, right):
    return jnp.dot(left, right, preferred_element_type=F32)


def outer_sum(left, right):
    return lax.dot_general(left, right, (((0,), (0,)), ((), ())), preferred_element_type=F32)


def times_transposed(left, right):
    return lax.dot_general(left, right, (((1,), (1,)), ((), ())), preferred_element_type=F32)


def flip(index, bit):
    return index + bit * (1 - 2 * ((index // bit) % 2))


def aligned(start, size, unit=16):
    if not isinstance(start, int):
        start = pl.multiple_of(start, unit)
    return pl.ds(start, size)


def remote(src, dst, sems, axis, target):
    return pltpu.make_async_remote_copy(
        src_ref=src,
        dst_ref=dst,
        send_sem=sems(),
        recv_sem=sems(),
        device_id={axis: target},
        device_id_type=MESH_ID,
    )


class Pool:
    def __init__(self, ref):
        self.ref, self.used = ref, 0

    def __call__(self):
        self.used += 1
        assert self.used <= SEMAPHORES
        return self.ref.at[self.used - 1]


class Place:
    def __init__(self):
        self.me = lax.axis_index("shard")
        self.rep = lax.axis_index("rep")
        self.core = flip(self.me, 1)
        self.chip = flip(self.me, 2)
        self.diagonal = flip(self.core, 2)


class AllGather:
    def __init__(self, place, sems, src, dst, tok, chunks):
        self.far, self.near, self.relays = [], [], []
        self.place, self.sems, self.dst, self.tok, self.chunks = place, sems, dst, tok, chunks
        size = tok // chunks
        for c in range(chunks):
            part = src.at[pl.ds(c * size, size)]
            self.far.append(remote(part, self.rows(place.me, c), sems, "shard", place.chip))
        for c in range(chunks):
            part = src.at[pl.ds(c * size, size)]
            self.near.append(remote(part, self.rows(place.me, c), sems, "shard", place.core))

    def rows(self, block, c):
        size = self.tok // self.chunks
        return self.dst.at[aligned(block * self.tok + c * size, size)]

    def start_far(self):
        for copy in self.far:
            copy.start()

    def start_near(self):
        for copy in self.near:
            copy.start()

    def relay(self, c):
        self.far[c].wait_recv()
        region = self.rows(self.place.chip, c)
        copy = remote(region, region, self.sems, "shard", self.place.core)
        copy.start()
        self.relays.append(copy)

    def relay_all(self):
        for c in range(self.chunks):
            self.relay(c)

    def finish_near(self):
        for copy in self.near:
            copy.wait_recv()

    def finish_far(self):
        for copy in self.relays:
            copy.wait_recv()

    def close(self):
        for copy in self.far + self.near + self.relays:
            copy.wait_send()


class ReduceScatter:
    def __init__(self, place, sems, part, near, outgoing, far, tok, chunks):
        self.place, self.sems, self.part, self.near = place, sems, part, near
        self.outgoing, self.far, self.tok, self.chunks = outgoing, far, tok, chunks
        self.size = tok // chunks
        self.first, self.second, self.third = [], [], []

    def rows(self, block, c):
        return aligned(block * self.tok + c * self.size, self.size)

    def piece(self, c):
        return pl.ds(c * self.size, self.size)

    def start(self, block, slot, copies):
        for c in range(self.chunks):
            copy = remote(
                self.part.at[self.rows(block, c)],
                self.near.at[slot, self.piece(c)],
                self.sems,
                "shard",
                self.place.core,
            )
            copy.start()
            copies.append(copy)

    def start_far(self):
        self.start(self.place.diagonal, 0, self.first)

    def start_near(self):
        self.start(self.place.core, 1, self.second)

    def forward(self):
        for c in range(self.chunks):
            self.first[c].wait_recv()
            piece = self.piece(c)
            mine = self.part[self.rows(self.place.chip, c)].astype(F32)
            self.outgoing[piece] = (mine + self.near[0, piece].astype(F32)).astype(B16)
            copy = remote(
                self.outgoing.at[piece], self.far.at[piece], self.sems, "shard", self.place.chip
            )
            copy.start()
            self.third.append(copy)

    def result(self):
        for copy in self.second + self.third:
            copy.wait_recv()
        mine = self.part[aligned(self.place.me * self.tok, self.tok)].astype(F32)
        return mine + self.near[1].astype(F32) + self.far[...].astype(F32)

    def close(self):
        for copy in self.first + self.second + self.third:
            copy.wait_send()


class Swap:
    def __init__(self, place, sems, source, packed, dest, kinds, relays):
        self.place, self.sems, self.source = place, sems, source
        self.packed, self.dest, self.kinds, self.relays = packed, dest, kinds, relays
        self.tall = source.shape[0]
        self.share = self.tall >> relays
        columns = dest.shape[1]
        cut = columns // LANES // 2 * LANES
        low = tuple(1 << i for i in range(relays))
        self.parts = []
        for first, size, order in ((0, cut, low), (cut, columns - cut, low[::-1])):
            position = 0
            for level, bit in enumerate(order):
                position = position + ((place.rep // bit) % 2) * (1 << level)
            self.parts.append((pl.ds(first, size), order, position))
        self.shared, self.whole = [], []

    def pack(self):
        blocks, _, columns = self.packed.shape
        size = columns // self.kinds
        for j in range(blocks):
            for kind in range(self.kinds):
                start = (kind * blocks + j) * size
                self.packed[j, :, kind * size : (kind + 1) * size] = self.source[
                    :, start : start + size
                ]

    def start_far(self):
        place = self.place
        for columns, order, position in self.parts:
            first = position * self.share
            for target in (place.chip, place.diagonal):
                copy = remote(
                    self.packed.at[target, aligned(first, self.share), columns],
                    self.dest.at[aligned(place.me * self.tall + first, self.share), columns],
                    self.sems,
                    "shard",
                    target,
                )
                copy.start()
                self.shared.append((target, columns, order, position, [copy]))

    def start_near(self):
        place = self.place
        mine = aligned(place.me * self.tall, self.tall)
        copy = remote(
            self.packed.at[place.core], self.dest.at[mine], self.sems, "shard", place.core
        )
        copy.start()
        self.whole.append(copy)
        self.dest[mine] = self.packed[place.me]

    def relay(self, level):
        if level >= self.relays:
            return
        for target, columns, order, position, copies in self.shared:
            copies[-1].wait_recv()
            length = self.share << level
            first = (position // (1 << level)) * length
            region = self.dest.at[aligned(target * self.tall + first, length), columns]
            copy = remote(region, region, self.sems, "rep", flip(self.place.rep, order[level]))
            copy.start()
            copies.append(copy)

    def finish(self):
        for entry in self.shared:
            entry[-1][-1].wait_recv()
        for copy in self.whole:
            copy.wait_recv()

    def close(self):
        for copy in self.whole:
            copy.wait_send()
        for entry in self.shared:
            for copy in entry[-1]:
                copy.wait_send()


def halves(order, index):
    length = 1 << len(order)
    offset = 0
    plan = []
    for bit in order:
        length //= 2
        side = (index // bit) % 2
        plan.append((bit, offset + side * length, offset + (1 - side) * length, length))
        offset = offset + side * length
    return plan


def streams_of(rows, n_rep):
    tiles = -(-rows // (16 * n_rep))
    low_first = tuple(1 << i for i in range(n_rep.bit_length() - 1))
    orders = (low_first, low_first[1::-1] + low_first[2:])
    first = min(tiles, -(-7 * tiles // 10))
    streams = []
    base = 0
    for share, order in zip((first, tiles - first), orders):
        if share:
            streams.append((base, 16 * share, order))
            base += 16 * share * n_rep
    return streams, base


class RepSum:
    def __init__(self, place, sems, streams, swap, acc, box, res):
        self.place, self.sems, self.streams, self.swap = place, sems, streams, swap
        self.acc, self.box, self.res = acc, box, res
        self.steps = len(streams[0][2])
        self.plans = [halves(order, place.rep) for _, _, order in streams]
        self.started = [[] for _ in streams]
        self.round = 0

    def at(self, ref, i, piece, length, lead=None):
        base, rows, _ = self.streams[i]
        span = aligned(base + piece * rows, length * rows)
        if not self.swap:
            return ref.at[span]
        return ref.at[slice(None) if lead is None else lead, span]

    def begin(self, i, k):
        plan, steps, place, sems = self.plans[i], self.steps, self.place, self.sems
        acc, box, res = self.acc, self.box, self.res
        if k < steps:
            bit, _, sent, length = plan[k]
            source, target = self.at(acc, i, sent, length), self.at(box, i, length, length)
            copies = [remote(source, target, sems, "rep", flip(place.rep, bit))]
        elif k == steps:
            mine = plan[-1][1]
            if not self.swap:
                copies = [
                    pltpu.make_async_copy(
                        self.at(acc, i, mine, 1), self.at(res, i, mine, 1), sems()
                    )
                ]
            else:
                target_block = self.at(res, i, mine, 1, place.me)
                copies = [
                    remote(self.at(acc, i, mine, 1, target), target_block, sems, "shard", target)
                    for target in (place.core, place.chip, place.diagonal)
                ]
                copies.append(
                    pltpu.make_async_copy(
                        self.at(acc, i, mine, 1, place.me), target_block, sems()
                    )
                )
        else:
            bit, kept, _, length = plan[2 * steps - k]
            region = self.at(res, i, kept, length)
            copies = [remote(region, region, sems, "rep", flip(place.rep, bit))]
        for copy in copies:
            copy.start()
        self.started[i].append(copies)

    def finish(self, i, k):
        copies = self.started[i][k]
        if k == self.steps:
            for copy in copies:
                copy.wait()
            return
        copies[0].wait_recv()
        if k > self.steps:
            return
        acc, box = self.acc, self.box
        base, rows, _ = self.streams[i]
        _, kept, _, length = self.plans[i][k]
        blocks = range(acc.shape[0]) if self.swap else (None,)

        @pl.loop(0, length)
        def _(p):
            to = aligned(base + (kept + p) * rows, rows)
            of = aligned(base + (length + p) * rows, rows)
            for block in blocks:
                x, y = ((to,), (of,)) if block is None else ((block, to), (block, of))
                acc[x] = (acc[x].astype(F32) + box[y].astype(F32)).astype(B16)

    def begin_all(self):
        for i in range(len(self.streams)):
            self.begin(i, 0)

    def advance(self):
        k = self.round
        if k > 2 * self.steps:
            return
        for i in range(len(self.streams)):
            self.finish(i, k)
            if k < 2 * self.steps:
                self.begin(i, k + 1)
        self.round += 1

    def done(self):
        return self.round > 2 * self.steps

    def close(self):
        for i in range(len(self.streams)):
            for k in range(2 * self.steps + 1):
                if k != self.steps:
                    self.started[i][k][0].wait_send()


class Total:
    def __init__(self, place, sems, sums, boxes, bits):
        self.place, self.sems, self.sums, self.boxes, self.bits = place, sems, sums, boxes, bits
        self.copies = []

    def begin(self):
        level = len(self.copies)
        axis, bit = self.bits[level]
        index = self.place.me if axis == "shard" else self.place.rep
        copy = remote(
            self.sums.at[level], self.boxes.at[level], self.sems, axis, flip(index, bit)
        )
        copy.start()
        self.copies.append(copy)

    def advance(self):
        level = len(self.copies) - 1
        if level >= len(self.bits):
            return
        self.copies[level].wait_recv()
        self.sums[level + 1] = self.sums[level] + self.boxes[level]
        if level + 1 < len(self.bits):
            self.begin()
        else:
            self.copies.append(None)

    def done(self):
        return len(self.copies) > len(self.bits)

    def close(self):
        for copy in self.copies[:-1]:
            copy.wait_send()


def pack_block(values, target, t):
    rows, columns = values.shape
    full, rest = divmod(columns, LANES)
    values = values.astype(B16)
    for j in range(full):
        target[t, j * rows : (j + 1) * rows] = values[:, j * LANES : (j + 1) * LANES]
    if rest:
        half = rows // 2
        tail = values[:, full * LANES :]
        target[t, full * rows : full * rows + half] = jnp.concatenate(
            [tail[:half], tail[half:]], axis=1
        )


def unpack_block(source, out, t, kinds):
    blocks = source.shape[0]
    rows, width = out.shape
    columns = width // blocks
    size = columns // kinds
    full, rest = divmod(columns, LANES)
    parts = [source[t, j * rows : (j + 1) * rows] for j in range(full)]
    if rest:
        tail = source[t, full * rows : full * rows + rows // 2]
        parts.append(jnp.concatenate([tail[:, :rest], tail[:, rest:]], axis=0))
    block = jnp.concatenate(parts, axis=1).astype(F32)
    for kind in range(kinds):
        start = (kind * blocks + t) * size
        out[:, start : start + size] = block[:, kind * size : (kind + 1) * size]


def pack_rows(values, target):
    rows = values.shape[0]
    values = values.astype(B16)
    for j in range(values.shape[1] // LANES):
        target[j * rows : (j + 1) * rows] = values[:, j * LANES : (j + 1) * LANES]


def unpack_rows(source, out):
    rows = out.shape[0]
    for j in range(out.shape[1] // LANES):
        out[:, j * LANES : (j + 1) * LANES] = source[j * rows : (j + 1) * rows].astype(F32)


def turned(values):
    lane = lax.broadcasted_iota(jnp.int32, values.shape, 1)
    half = HEAD_DIM // 2
    ahead = pltpu.roll(values, LANES - half, 1)
    behind = pltpu.roll(values, half, 1)
    return jnp.where(lane % HEAD_DIM < half, ahead, behind)


def query_scale(tile, part, rows):
    lane = lax.broadcasted_iota(jnp.int32, (rows, LANES), 1) + tile * LANES
    return jnp.where(lane < part, HEAD_DIM ** (-0.5), 1.0)


class Config:
    pass


def layer_kernel(cfg, *refs):
    r = Config()
    r.__dict__.update(zip(cfg.names, refs))
    r.__dict__.update(jax.tree.unflatten(cfg.tree, refs[len(cfg.names) :]))
    tok, width, part, heads, hidden = cfg.tok, cfg.width, cfg.part, cfg.heads, cfg.hidden
    n_shard, count, chunks = cfg.n_shard, cfg.count, cfg.chunks
    place = Place()
    sems = Pool(r.sems)
    me, core, chip, diagonal = place.me, place.core, place.chip, place.diagonal
    rep_bits = [1 << b for b in range(cfg.n_rep.bit_length() - 1)]
    partners = [("shard", core), ("shard", chip), ("shard", diagonal)]
    partners += [("rep", flip(place.rep, bit)) for bit in rep_bits]
    barrier = pltpu.get_barrier_semaphore()
    for axis, target in partners:
        pl.semaphore_signal(barrier, inc=1, device_id={axis: target}, device_id_type=MESH_ID)
    own = aligned(me * tok, tok)
    half = count // 2
    near_start = (me // 2) * half
    far_start = (chip // 2) * half

    qkv = Swap(place, sems, r.qkv, r.pk_qkv, r.w_qkv, 3, cfg.relays)
    win = Swap(place, sems, r.win, r.pk_in, r.w_in, 2, cfg.relays)
    tokens = AllGather(place, sems, r.tokens, r.toks, tok, chunks)
    grads = AllGather(place, sems, r.grad, r.grads, tok, chunks)
    gains = [
        remote(r.gains, r.all_gains.at[me], sems, "shard", target)
        for target in (core, chip, diagonal)
    ]
    qkv.pack()
    pl.semaphore_wait(barrier, len(partners))
    qkv.start_far()
    tokens.start_far()
    for copy in gains:
        copy.start()
    tokens.start_near()
    qkv.start_near()
    r.toks[own] = r.tokens[...]
    r.grads[own] = r.grad[...]
    r.all_gains[me] = r.gains[...]
    win.pack()
    for name, rows in cfg.padding:
        acc = r.acc[name]
        if len(acc.shape) == 3:
            acc[:, rows:] = jnp.zeros((n_shard, acc.shape[1] - rows, LANES), B16)
        else:
            acc[rows:] = jnp.zeros((acc.shape[0] - rows, LANES), B16)
    normed, inverse = normalize(r.tokens[...].astype(F32))
    r.xhat1[...] = normed
    r.inv1[...] = inverse
    r.sums[0] = jnp.zeros((16, LANES), F32)
    for copy in gains:
        copy.wait_recv()
    for t in range(n_shard):
        columns = slice(t * part, (t + 1) * part)
        r.gain1[:, columns] = r.all_gains[t, 0:1].astype(F32)
        r.gain2[:, columns] = r.all_gains[t, 1:2].astype(F32)

    def normalize_half(start):
        @pl.loop(0, half // tok)
        def _(i):
            rows = aligned(start + i * tok, tok)
            values, _ = normalize(r.toks[rows].astype(F32))
            r.h1[rows] = (values * r.gain1[...]).astype(B16)

    tokens.finish_near()
    normalize_half(near_start)
    qkv.relay(0)
    tokens.relay_all()
    qkv.relay(1)
    grads.start_far()
    grads.start_near()
    win.start_far()
    win.start_near()
    tokens.finish_far()
    normalize_half(far_start)
    qkv.finish()

    @pl.loop(0, 2)
    def _(i):
        rows = aligned(i * half, half)
        projected = dot(r.h1[rows], r.w_qkv[...])
        cosine, sine = r.cosine[rows], r.sine[rows]
        for j in range(3 * part // LANES + 1):
            size = min(LANES, 3 * part - j * LANES)
            tile = projected[:, j * LANES : j * LANES + size]
            if (j + 1) * LANES <= 2 * part:
                tile = tile * cosine + turned(tile) * sine
                if j * LANES < part:
                    tile = tile * query_scale(j, part, half)
            tile = tile.astype(B16)
            for k in range(size // HEAD_DIM):
                index = j * (LANES // HEAD_DIM) + k
                r.heads[index, rows] = tile[:, k * HEAD_DIM : (k + 1) * HEAD_DIM]

    win.relay(0)
    grads.relay_all()

    @pl.loop(0, heads)
    def _(h):
        key, value = r.heads[heads + h], r.heads[2 * heads + h]
        for b in range(2):
            rows = pl.ds(b * half, half)
            scores = times_transposed(r.heads[h, rows], key)
            maxima = jnp.max(scores, axis=-1, keepdims=True)
            expo = jnp.exp(scores - maxima)
            total = jnp.sum(expo, axis=-1, keepdims=True)
            probs = (expo * (1.0 / total)).astype(B16)
            r.probs[h, rows] = probs
            r.att_heads[h, rows] = dot(probs, value).astype(B16)

    for h in range(heads):
        r.att[:, h * HEAD_DIM : (h + 1) * HEAD_DIM] = r.att_heads[h]

    def reduce(name):
        return ReduceScatter(
            place, sems, r.parts[name], r.nears[name], r.outgoing[name], r.fars[name], tok, chunks
        )

    def project(start):
        rows = aligned(start, half)
        r.parts["att"][rows] = dot(r.att[rows], r.w_out[...]).astype(B16)

    mixed = reduce("att")
    project(far_start)
    mixed.start_far()
    project(near_start)
    mixed.start_near()
    win.relay(1)
    mixed.forward()
    resid = r.tokens[...].astype(F32) + mixed.result()
    r.resid[...] = resid
    normed, inverse = normalize(resid)
    r.xhat2[...] = normed
    r.inv2[...] = inverse
    scaled = (normed * r.gain2[...]).astype(B16)
    r.h2[own] = scaled
    second = AllGather(place, sems, r.h2.at[own], r.h2, tok, chunks)
    second.start_far()
    second.start_near()
    win.finish()
    grads.finish_near()
    grads.finish_far()

    def feed_forward(start):
        rows = aligned(start, half)
        upper = dot(r.h2[rows], r.w_in[...])
        inner, gate = upper[:, :hidden], upper[:, hidden:]
        value, slope = gelu_pair(inner)
        act = (value * gate).astype(B16)
        r.act[rows] = act
        grad_act = times_transposed(r.grads[rows], r.down[...])
        grad_upper = jnp.concatenate(
            [grad_act * gate * slope, grad_act * value], axis=-1
        ).astype(B16)
        r.gup[rows] = grad_upper
        r.parts["h2"][rows] = times_transposed(grad_upper, r.w_in[...]).astype(B16)
        r.parts["down"][rows] = dot(act, r.down[...]).astype(B16)

    back2, down = reduce("h2"), reduce("down")
    second.finish_near()
    feed_forward(near_start)
    back2.start_near()
    second.relay_all()
    second.finish_far()
    feed_forward(far_start)
    back2.start_far()
    down.start_near()
    down.start_far()

    groups = {}
    for name, streams, swap in cfg.groups:
        groups[name] = RepSum(
            place, sems, streams, swap, r.acc[name], r.box[name], r.res[name]
        )
    active = []

    def launch(name):
        groups[name].begin_all()
        active.append(groups[name])

    def pump():
        for item in active:
            if not item.done():
                item.advance()

    pack_rows(outer_sum(r.act[...], r.grads[...]), r.acc["down"])
    launch("down")
    back2.forward()

    def pack_pairs(left, right, target):
        for i in range(n_shard // 2):
            columns = slice(i * 2 * part, (i + 1) * 2 * part)
            values = outer_sum(left[:, columns], right[...])
            pack_block(values[:part], target, 2 * i)
            pack_block(values[part:], target, 2 * i + 1)

    pack_pairs(r.h2, r.gup, r.acc["in"])
    launch("in")
    grad_h2 = back2.result()
    back, gain_grad = norm_backward(grad_h2, r.xhat2[...], r.inv2[...], r.gain2[...])
    for j in range(width // LANES):
        r.sums[0, 8 + j : 9 + j] = gain_grad[:, j * LANES : (j + 1) * LANES]
    grad_resid = r.grad[...].astype(F32) + back
    r.gres[...] = grad_resid
    r.resid_b[own] = grad_resid.astype(B16)
    third = AllGather(place, sems, r.resid_b.at[own], r.resid_b, tok, chunks)
    third.start_far()
    third.start_near()
    down.forward()
    pump()

    def attention_grad(start):
        rows = aligned(start, half)
        values = times_transposed(r.resid_b[rows], r.w_out[...]).astype(B16)
        for h in range(heads):
            r.gatt[h, rows] = values[:, h * HEAD_DIM : (h + 1) * HEAD_DIM]

    third.finish_near()
    attention_grad(near_start)
    third.relay_all()
    third.finish_far()
    attention_grad(far_start)
    pack_rows(outer_sum(r.att[...], r.resid_b[...]), r.acc["out"])
    launch("out")

    @pl.loop(0, heads)
    def _(h):
        key, value, query = r.heads[heads + h], r.heads[2 * heads + h], r.heads[h]
        grad_value = jnp.zeros((count, HEAD_DIM), F32)
        grad_key = jnp.zeros((count, HEAD_DIM), F32)
        for b in range(2):
            rows = pl.ds(b * half, half)
            grad_head = r.gatt[h, rows]
            probs = r.probs[h, rows]
            attended = r.att_heads[h, rows].astype(F32)
            delta = jnp.sum(grad_head.astype(F32) * attended, axis=-1, keepdims=True)
            grad_value = grad_value + outer_sum(probs, grad_head)
            grad_probs = times_transposed(grad_head, value)
            grad_scores = (probs.astype(F32) * (grad_probs - delta)).astype(B16)
            r.gheads[h, rows] = dot(grad_scores, key)
            grad_key = grad_key + outer_sum(grad_scores, query[b * half : (b + 1) * half])
        r.gheads[heads + h] = grad_key
        r.gheads[2 * heads + h] = grad_value

    pump()
    grad_parts = reduce("h1")

    def project_back(start):
        rows = aligned(start, half)
        cosine, sine = r.cosine[rows], r.sine[rows]
        for j in range(3 * part // LANES + 1):
            size = min(LANES, 3 * part - j * LANES)
            index = j * (LANES // HEAD_DIM)
            tile = jnp.concatenate(
                [r.gheads[index + k, rows] for k in range(size // HEAD_DIM)], axis=-1
            )
            if (j + 1) * LANES <= 2 * part:
                tile = tile * cosine - turned(tile) * sine
                if j * LANES < part:
                    tile = tile * query_scale(j, part, half)
            r.gproj[rows, j * LANES : j * LANES + size] = tile.astype(B16)
        r.parts["h1"][rows] = times_transposed(r.gproj[rows], r.w_qkv[...]).astype(B16)

    project_back(far_start)
    grad_parts.start_far()
    project_back(near_start)
    grad_parts.start_near()
    pack_pairs(r.h1, r.gproj, r.acc["qkv"])
    launch("qkv")
    grad_parts.forward()
    r.o_output[...] = (r.resid[...] + down.result()).astype(B16)
    pump()
    grad_h1 = grad_parts.result()
    back, gain_grad = norm_backward(grad_h1, r.xhat1[...], r.inv1[...], r.gain1[...])
    for j in range(width // LANES):
        r.sums[0, j : j + 1] = gain_grad[:, j * LANES : (j + 1) * LANES]
    small = Total(
        place, sems, r.sums, r.boxes,
        [("shard", 1), ("shard", 2)] + [("rep", bit) for bit in rep_bits],
    )
    small.begin()
    active.append(small)
    r.o_tokens[...] = r.gres[...] + back
    while not all(item.done() for item in active):
        pump()
    total = r.sums[len(small.bits)]
    for out, at in ((r.o_gain1, 0), (r.o_gain2, 8)):
        row = jnp.concatenate(
            [total[at + j : at + j + 1] for j in range(width // LANES)], axis=1
        )
        picked = jnp.zeros((1, part), F32)
        for t in range(n_shard):
            picked = jnp.where(me == t, row[:, t * part : (t + 1) * part], picked)
        out[...] = picked
    unpack_rows(r.res["down"], r.o_down)
    unpack_rows(r.res["out"], r.o_out)
    for t in range(n_shard):
        unpack_block(r.res["in"], r.o_in, t, 2)
        unpack_block(r.res["qkv"], r.o_qkv, t, 3)
    for copy in gains:
        copy.wait_send()
    for item in [qkv, win, tokens, grads, second, third, mixed, back2, down, grad_parts]:
        item.close()
    for item in active:
        item.close()


def rotary_tables(count):
    half = HEAD_DIM // 2
    freq = THETA ** (-np.arange(half, dtype=np.float64) * 2.0 / HEAD_DIM)
    angles = np.arange(count, dtype=np.float64)[:, None] * freq[None, :]
    angles = np.concatenate([angles, angles], axis=-1)
    sign = np.where(np.arange(HEAD_DIM) < half, -1.0, 1.0)
    repeat = LANES // HEAD_DIM
    cosine = np.tile(np.cos(angles), (1, repeat))
    sine = np.tile(np.sin(angles) * sign, (1, repeat))
    return cosine.astype(np.float32), sine.astype(np.float32)


def local(
    n_shard, n_rep, tokens, gain_one, qkv_weight, out_weight, gain_two, in_weight, down_weight,
    grad_output
):
    tok, width = tokens.shape[1:]
    cfg = Config()
    cfg.n_shard, cfg.n_rep, cfg.tok, cfg.width = n_shard, n_rep, tok, width
    cfg.part = part = width // n_shard
    cfg.heads = heads = part // HEAD_DIM
    cfg.hidden = hidden = down_weight.shape[0]
    cfg.count = count = tok * n_shard
    cfg.chunks = 2
    cfg.relays = min(2, n_rep.bit_length() - 1)
    while cfg.relays and part % (16 << cfg.relays):
        cfg.relays -= 1
    cosine, sine = rotary_tables(count)
    ins = dict(
        tokens=tokens.reshape(tok, width),
        gains=jnp.stack([gain_one, gain_two]),
        qkv=qkv_weight,
        w_out=out_weight,
        win=in_weight,
        down=down_weight,
        grad=grad_output.reshape(tok, width),
        cosine=jnp.asarray(cosine),
        sine=jnp.asarray(sine),
    )
    outs = dict(
        o_output=((tok, width), B16),
        o_tokens=((tok, width), F32),
        o_gain1=((1, part), F32),
        o_qkv=((part, 3 * width), F32),
        o_out=((part, width), F32),
        o_gain2=((1, part), F32),
        o_in=((part, 2 * hidden * n_shard), F32),
        o_down=((hidden, width), F32),
    )
    scratch = dict(
        toks=((count, width), B16),
        grads=((count, width), B16),
        all_gains=((n_shard, 2, part), B16),
        gain1=((1, width), F32),
        gain2=((1, width), F32),
        pk_qkv=((n_shard, part, 3 * part), B16),
        w_qkv=((width, 3 * part), B16),
        pk_in=((n_shard, part, 2 * hidden), B16),
        w_in=((width, 2 * hidden), B16),
        h1=((count, width), B16),
        heads=((3 * heads, count, HEAD_DIM), B16),
        probs=((heads, count, count), B16),
        att_heads=((heads, count, HEAD_DIM), B16),
        att=((count, part), B16),
        h2=((count, width), B16),
        act=((count, hidden), B16),
        gup=((count, 2 * hidden), B16),
        resid=((tok, width), F32),
        xhat1=((tok, width), F32),
        inv1=((tok, 1), F32),
        xhat2=((tok, width), F32),
        inv2=((tok, 1), F32),
        gres=((tok, width), F32),
        resid_b=((count, width), B16),
        gatt=((heads, count, HEAD_DIM), B16),
        gheads=((3 * heads, count, HEAD_DIM), F32),
        gproj=((count, 3 * part), B16),
        sums=((n_rep.bit_length() + 2, 16, LANES), F32),
        boxes=((n_rep.bit_length() + 1, 16, LANES), F32),
    )
    exchanges = ("att", "h2", "down", "h1")
    scratch.update(
        parts={name: ((count, width), B16) for name in exchanges},
        nears={name: ((2, tok, width), B16) for name in exchanges},
        outgoing={name: ((tok, width), B16) for name in exchanges},
        fars={name: ((tok, width), B16) for name in exchanges},
    )
    cfg.groups, cfg.padding, padded = [], [], {}
    for name, rows, swap in (
        ("down", hidden * width // LANES, False),
        ("in", part * 2 * hidden // LANES, True),
        ("out", part * width // LANES, False),
        ("qkv", part * 3 * part // LANES, True),
    ):
        streams, tall = streams_of(rows, n_rep)
        cfg.groups.append((name, streams, swap))
        if tall > rows:
            cfg.padding.append((name, rows))
        padded[name] = ((n_shard, tall, LANES) if swap else (tall, LANES), B16)
    scratch.update(acc=padded, box=padded, res=padded)

    def is_entry(item):
        return isinstance(item, tuple)

    spaces = jax.tree.map(lambda entry: pltpu.VMEM(*entry), scratch, is_leaf=is_entry)
    spaces["sems"] = pltpu.SemaphoreType.DMA((SEMAPHORES,))
    spaces, cfg.tree = jax.tree.flatten(spaces)
    cfg.names = list(ins) + list(outs)
    results = pl.pallas_call(
        functools.partial(layer_kernel, cfg),
        out_shape=tuple(jax.ShapeDtypeStruct(*entry) for entry in outs.values()),
        in_specs=[VMEM] * len(ins),
        out_specs=tuple([VMEM] * len(outs)),
        scratch_shapes=spaces,
        compiler_params=pltpu.CompilerParams(
            collective_id=0, has_side_effects=True, vmem_limit_bytes=63 * 1024 * 1024
        ),
    )(*ins.values())
    output, grad_tokens, gain1, grad_qkv, grad_out, gain2, grad_in, grad_down = results
    return (
        output.reshape(1, tok, width),
        grad_tokens.reshape(1, tok, width),
        gain1.reshape(part),
        grad_qkv,
        grad_out,
        gain2.reshape(part),
        grad_in,
        grad_down,
    )


def solution(mesh):
    in_specs = (
        P("rep", "shard", None),
        P("shard"),
        P("shard", None),
        P("shard", None),
        P("shard"),
        P("shard", None),
        P("shard", None),
        P("rep", "shard", None),
    )
    out_specs = (
        P("rep", "shard", None),
        P("rep", "shard", None),
        P("shard"),
        P("shard", None),
        P("shard", None),
        P("shard"),
        P("shard", None),
        P("shard", None),
    )
    body = functools.partial(local, mesh.shape["shard"], mesh.shape["rep"])
    return jax.shard_map(body, mesh=mesh, in_specs=in_specs, out_specs=out_specs, check_vma=False)
```

```python
import functools

import jax
import jax.numpy as jnp
import numpy as np
from jax import lax
from jax.experimental import pallas as pl
from jax.experimental.pallas import tpu as pltpu
from jax.sharding import PartitionSpec as P

HEAD_DIM = 64
EPSILON = 1e-05
THETA = 160000.0
SQRT_HALF = 0.7071067811865476
INV_SQRT_TAU = 0.3989422804014327
MESH_ID = pl.DeviceIdType.MESH
LANES = 128
VMEM = pl.BlockSpec(memory_space=pltpu.VMEM)
F32 = jnp.float32
B16 = jnp.bfloat16
SEMAPHORES = 448


def normalize(values):
    mean_row = jnp.mean(values, axis=-1, keepdims=True)
    centred = values - mean_row
    variance = jnp.mean(centred * centred, axis=-1, keepdims=True)
    inverse = lax.rsqrt(variance + EPSILON)
    return (centred * inverse, inverse)


def norm_backward(grad_out, normed, inverse, gain):
    grad_normed = grad_out * gain
    gain_grad = jnp.sum(grad_out * normed, axis=0, keepdims=True)
    first = jnp.mean(grad_normed, axis=-1, keepdims=True)
    second = jnp.mean(grad_normed * normed, axis=-1, keepdims=True)
    return (inverse * (grad_normed - first - normed * second), gain_grad)


def gelu_pair(inner):
    cdf = 0.5 * (1.0 + lax.erf(inner * SQRT_HALF))
    return (inner * cdf, cdf + inner * jnp.exp(-0.5 * inner * inner) * INV_SQRT_TAU)


def dot(left, right):
    return jnp.dot(left, right, preferred_element_type=F32)


def outer_sum(left, right):
    return lax.dot_general(left, right, (((0,), (0,)), ((), ())), preferred_element_type=F32)


def times_transposed(left, right):
    return lax.dot_general(left, right, (((1,), (1,)), ((), ())), preferred_element_type=F32)


def flip(index, bit):
    return index + bit * (1 - 2 * ((index // bit) % 2))


def aligned(start, size, unit=16):
    if not isinstance(start, int):
        start = pl.multiple_of(start, unit)
    return pl.ds(start, size)


def remote(src, dst, sems, axis, target):
    return pltpu.make_async_remote_copy(
        src_ref=src,
        dst_ref=dst,
        send_sem=sems(),
        recv_sem=sems(),
        device_id={axis: target},
        device_id_type=MESH_ID,
    )


class Pool:
    def __init__(self, ref):
        self.ref, self.used = ref, 0

    def __call__(self):
        self.used += 1
        assert self.used <= SEMAPHORES
        return self.ref.at[self.used - 1]


class Place:
    def __init__(self):
        self.me = lax.axis_index("shard")
        self.rep = lax.axis_index("rep")
        self.core = flip(self.me, 1)
        self.chip = flip(self.me, 2)
        self.diagonal = flip(self.core, 2)


class AllGather:
    def __init__(self, place, sems, src, dst, tok, chunks):
        self.far, self.near, self.relays = [], [], []
        self.place, self.sems, self.dst, self.tok, self.chunks = place, sems, dst, tok, chunks
        size = tok // chunks
        for c in range(chunks):
            part = src.at[pl.ds(c * size, size)]
            self.far.append(remote(part, self.rows(place.me, c), sems, "shard", place.chip))
        for c in range(chunks):
            part = src.at[pl.ds(c * size, size)]
            self.near.append(remote(part, self.rows(place.me, c), sems, "shard", place.core))

    def rows(self, block, c):
        size = self.tok // self.chunks
        return self.dst.at[aligned(block * self.tok + c * size, size)]

    def start_far(self):
        for copy in self.far:
            copy.start()

    def start_near(self):
        for copy in self.near:
            copy.start()

    def relay(self, c):
        self.far[c].wait_recv()
        region = self.rows(self.place.chip, c)
        copy = remote(region, region, self.sems, "shard", self.place.core)
        copy.start()
        self.relays.append(copy)

    def relay_all(self):
        for c in range(self.chunks):
            self.relay(c)

    def finish_near(self):
        for copy in self.near:
            copy.wait_recv()

    def finish_far(self):
        for copy in self.relays:
            copy.wait_recv()

    def close(self):
        for copy in self.far + self.near + self.relays:
            copy.wait_send()


class ReduceScatter:
    def __init__(self, place, sems, part, near, outgoing, far, tok, chunks):
        self.place, self.sems, self.part, self.near = place, sems, part, near
        self.outgoing, self.far, self.tok, self.chunks = outgoing, far, tok, chunks
        self.size = tok // chunks
        self.first, self.second, self.third = [], [], []

    def rows(self, block, c):
        return aligned(block * self.tok + c * self.size, self.size)

    def piece(self, c):
        return pl.ds(c * self.size, self.size)

    def start(self, block, slot, copies):
        for c in range(self.chunks):
            copy = remote(
                self.part.at[self.rows(block, c)],
                self.near.at[slot, self.piece(c)],
                self.sems,
                "shard",
                self.place.core,
            )
            copy.start()
            copies.append(copy)

    def start_far(self):
        self.start(self.place.diagonal, 0, self.first)

    def start_near(self):
        self.start(self.place.core, 1, self.second)

    def forward(self):
        for c in range(self.chunks):
            self.first[c].wait_recv()
            piece = self.piece(c)
            mine = self.part[self.rows(self.place.chip, c)].astype(F32)
            self.outgoing[piece] = (mine + self.near[0, piece].astype(F32)).astype(B16)
            copy = remote(
                self.outgoing.at[piece], self.far.at[piece], self.sems, "shard", self.place.chip
            )
            copy.start()
            self.third.append(copy)

    def result(self):
        for copy in self.second + self.third:
            copy.wait_recv()
        mine = self.part[aligned(self.place.me * self.tok, self.tok)].astype(F32)
        return mine + self.near[1].astype(F32) + self.far[...].astype(F32)

    def close(self):
        for copy in self.first + self.second + self.third:
            copy.wait_send()


class Swap:
    def __init__(self, place, sems, source, packed, dest, kinds, relays):
        self.place, self.sems, self.source = place, sems, source
        self.packed, self.dest, self.kinds, self.relays = packed, dest, kinds, relays
        self.tall = source.shape[0]
        self.share = self.tall >> relays
        columns = dest.shape[1]
        cut = columns // LANES // 2 * LANES
        low = tuple(1 << i for i in range(relays))
        self.parts = []
        for first, size, order in ((0, cut, low), (cut, columns - cut, low[::-1])):
            position = 0
            for level, bit in enumerate(order):
                position = position + ((place.rep // bit) % 2) * (1 << level)
            self.parts.append((pl.ds(first, size), order, position))
        self.shared, self.whole = [], []

    def pack(self):
        blocks, _, columns = self.packed.shape
        size = columns // self.kinds
        for j in range(blocks):
            for kind in range(self.kinds):
                start = (kind * blocks + j) * size
                self.packed[j, :, kind * size : (kind + 1) * size] = self.source[
                    :, start : start + size
                ]

    def start_far(self):
        place = self.place
        for columns, order, position in self.parts:
            first = position * self.share
            for target in (place.chip, place.diagonal):
                copy = remote(
                    self.packed.at[target, aligned(first, self.share), columns],
                    self.dest.at[aligned(place.me * self.tall + first, self.share), columns],
                    self.sems,
                    "shard",
                    target,
                )
                copy.start()
                self.shared.append((target, columns, order, position, [copy]))

    def start_near(self):
        place = self.place
        mine = aligned(place.me * self.tall, self.tall)
        copy = remote(
            self.packed.at[place.core], self.dest.at[mine], self.sems, "shard", place.core
        )
        copy.start()
        self.whole.append(copy)
        self.dest[mine] = self.packed[place.me]

    def relay(self, level):
        if level >= self.relays:
            return
        for target, columns, order, position, copies in self.shared:
            copies[-1].wait_recv()
            length = self.share << level
            first = (position // (1 << level)) * length
            region = self.dest.at[aligned(target * self.tall + first, length), columns]
            copy = remote(region, region, self.sems, "rep", flip(self.place.rep, order[level]))
            copy.start()
            copies.append(copy)

    def finish(self):
        for entry in self.shared:
            entry[-1][-1].wait_recv()
        for copy in self.whole:
            copy.wait_recv()

    def close(self):
        for copy in self.whole:
            copy.wait_send()
        for entry in self.shared:
            for copy in entry[-1]:
                copy.wait_send()


def halves(order, index):
    length = 1 << len(order)
    offset = 0
    plan = []
    for bit in order:
        length //= 2
        side = (index // bit) % 2
        plan.append((bit, offset + side * length, offset + (1 - side) * length, length))
        offset = offset + side * length
    return plan


def streams_of(rows, n_rep):
    tiles = -(-rows // (16 * n_rep))
    low_first = tuple(1 << i for i in range(n_rep.bit_length() - 1))
    second = low_first[1::-1] + low_first[2:]
    early = -(-5 * tiles // 7)
    shares = ((-(-early // 2), low_first), (early // 2, low_first), (tiles - early, second))
    streams = []
    base = 0
    for share, order in shares:
        if share:
            streams.append((base, 16 * share, order))
            base += 16 * share * n_rep
    return streams, base


class RepSum:
    def __init__(self, place, sems, stream, swap, acc, box, res):
        self.place, self.sems, self.swap = place, sems, swap
        self.base, self.rows, order = stream
        self.acc, self.box, self.res = acc, box, res
        self.steps = len(order)
        self.plan = halves(order, place.rep)
        self.started = []
        self.round = 0

    def at(self, ref, piece, length, lead=None):
        span = aligned(self.base + piece * self.rows, length * self.rows)
        if not self.swap:
            return ref.at[span]
        return ref.at[slice(None) if lead is None else lead, span]

    def begin(self):
        k, plan, steps, place, sems = self.round, self.plan, self.steps, self.place, self.sems
        acc, box, res = self.acc, self.box, self.res
        if k < steps:
            bit, _, sent, length = plan[k]
            source, target = self.at(acc, sent, length), self.at(box, length, length)
            copies = [remote(source, target, sems, "rep", flip(place.rep, bit))]
        elif k == steps:
            mine = plan[-1][1]
            if not self.swap:
                copies = [
                    pltpu.make_async_copy(self.at(acc, mine, 1), self.at(res, mine, 1), sems())
                ]
            else:
                target_block = self.at(res, mine, 1, place.me)
                copies = [
                    remote(self.at(acc, mine, 1, target), target_block, sems, "shard", target)
                    for target in (place.core, place.chip, place.diagonal)
                ]
                copies.append(
                    pltpu.make_async_copy(self.at(acc, mine, 1, place.me), target_block, sems())
                )
        else:
            bit, kept, _, length = plan[2 * steps - k]
            region = self.at(res, kept, length)
            copies = [remote(region, region, sems, "rep", flip(place.rep, bit))]
        for copy in copies:
            copy.start()
        self.started.append(copies)

    def finish(self):
        k = self.round
        copies = self.started[k]
        if k == self.steps:
            for copy in copies:
                copy.wait()
            return
        copies[0].wait_recv()
        if k > self.steps:
            return
        acc, box, base, rows = self.acc, self.box, self.base, self.rows
        _, kept, _, length = self.plan[k]
        blocks = range(acc.shape[0]) if self.swap else (None,)

        @pl.loop(0, length)
        def _(p):
            to = aligned(base + (kept + p) * rows, rows)
            of = aligned(base + (length + p) * rows, rows)
            for block in blocks:
                x, y = ((to,), (of,)) if block is None else ((block, to), (block, of))
                acc[x] = (acc[x].astype(F32) + box[y].astype(F32)).astype(B16)

    def advance(self):
        self.finish()
        self.round += 1
        if not self.done():
            self.begin()

    def done(self):
        return self.round > 2 * self.steps

    def close(self):
        for k in range(2 * self.steps + 1):
            if k != self.steps:
                self.started[k][0].wait_send()


class Total:
    def __init__(self, place, sems, sums, boxes, bits):
        self.place, self.sems, self.sums, self.boxes, self.bits = place, sems, sums, boxes, bits
        self.copies = []

    def begin(self):
        level = len(self.copies)
        axis, bit = self.bits[level]
        index = self.place.me if axis == "shard" else self.place.rep
        copy = remote(
            self.sums.at[level], self.boxes.at[level], self.sems, axis, flip(index, bit)
        )
        copy.start()
        self.copies.append(copy)

    def advance(self):
        level = len(self.copies) - 1
        if level >= len(self.bits):
            return
        self.copies[level].wait_recv()
        self.sums[level + 1] = self.sums[level] + self.boxes[level]
        if level + 1 < len(self.bits):
            self.begin()
        else:
            self.copies.append(None)

    def done(self):
        return len(self.copies) > len(self.bits)

    def close(self):
        for copy in self.copies[:-1]:
            copy.wait_send()


def pack_block(values, target, t):
    rows, columns = values.shape
    full, rest = divmod(columns, LANES)
    values = values.astype(B16)
    for j in range(full):
        target[t, j * rows : (j + 1) * rows] = values[:, j * LANES : (j + 1) * LANES]
    if rest:
        half = rows // 2
        tail = values[:, full * LANES :]
        target[t, full * rows : full * rows + half] = jnp.concatenate(
            [tail[:half], tail[half:]], axis=1
        )


def unpack_block(source, out, t, kinds):
    blocks = source.shape[0]
    rows, width = out.shape
    columns = width // blocks
    size = columns // kinds
    full, rest = divmod(columns, LANES)
    parts = [source[t, j * rows : (j + 1) * rows] for j in range(full)]
    if rest:
        tail = source[t, full * rows : full * rows + rows // 2]
        parts.append(jnp.concatenate([tail[:, :rest], tail[:, rest:]], axis=0))
    block = jnp.concatenate(parts, axis=1).astype(F32)
    for kind in range(kinds):
        start = (kind * blocks + t) * size
        out[:, start : start + size] = block[:, kind * size : (kind + 1) * size]


def pack_rows(values, target):
    rows = values.shape[0]
    values = values.astype(B16)
    for j in range(values.shape[1] // LANES):
        target[j * rows : (j + 1) * rows] = values[:, j * LANES : (j + 1) * LANES]


def unpack_rows(source, out):
    rows = out.shape[0]
    for j in range(out.shape[1] // LANES):
        out[:, j * LANES : (j + 1) * LANES] = source[j * rows : (j + 1) * rows].astype(F32)


def turned(values):
    lane = lax.broadcasted_iota(jnp.int32, values.shape, 1)
    half = HEAD_DIM // 2
    ahead = pltpu.roll(values, LANES - half, 1)
    behind = pltpu.roll(values, half, 1)
    return jnp.where(lane % HEAD_DIM < half, ahead, behind)


def query_scale(tile, part, rows):
    lane = lax.broadcasted_iota(jnp.int32, (rows, LANES), 1) + tile * LANES
    return jnp.where(lane < part, HEAD_DIM ** (-0.5), 1.0)


class Config:
    pass


def layer_kernel(cfg, *refs):
    r = Config()
    r.__dict__.update(zip(cfg.names, refs))
    refs = refs[len(cfg.names) :]
    r.res = dict(zip(cfg.sums, refs))
    r.__dict__.update(jax.tree.unflatten(cfg.tree, refs[len(cfg.sums) :]))
    tok, width, part, heads, hidden = cfg.tok, cfg.width, cfg.part, cfg.heads, cfg.hidden
    n_shard, count, chunks = cfg.n_shard, cfg.count, cfg.chunks
    place = Place()
    sems = Pool(r.sems)
    me, core, chip, diagonal = place.me, place.core, place.chip, place.diagonal
    rep_bits = [1 << b for b in range(cfg.n_rep.bit_length() - 1)]
    partners = [("shard", core), ("shard", chip), ("shard", diagonal)]
    partners += [("rep", flip(place.rep, bit)) for bit in rep_bits]
    barrier = pltpu.get_barrier_semaphore()
    for axis, target in partners:
        pl.semaphore_signal(barrier, inc=1, device_id={axis: target}, device_id_type=MESH_ID)
    own = aligned(me * tok, tok)
    half = count // 2
    near_start = (me // 2) * half
    far_start = (chip // 2) * half

    qkv = Swap(place, sems, r.qkv, r.pk_qkv, r.w_qkv, 3, cfg.relays)
    win = Swap(place, sems, r.win, r.pk_in, r.w_in, 2, cfg.relays)
    tokens = AllGather(place, sems, r.tokens, r.toks, tok, chunks)
    grads = AllGather(place, sems, r.grad, r.grads, tok, chunks)
    gains = [
        remote(r.gains, r.all_gains.at[me], sems, "shard", target)
        for target in (core, chip, diagonal)
    ]
    r.gains[0:1] = r.gain_one[...].reshape(1, part)
    r.gains[1:2] = r.gain_two[...].reshape(1, part)
    qkv.pack()
    pl.semaphore_wait(barrier, len(partners))
    for copy in gains:
        copy.start()
    qkv.start_far()
    tokens.start_far()
    tokens.start_near()
    qkv.start_near()
    r.toks[own] = r.tokens[...]
    r.grads[own] = r.grad[...]
    r.all_gains[me] = r.gains[...]
    win.pack()
    for name, rows in cfg.padding:
        acc = r.acc[name]
        if len(acc.shape) == 3:
            acc[:, rows:] = jnp.zeros((n_shard, acc.shape[1] - rows, LANES), B16)
        else:
            acc[rows:] = jnp.zeros((acc.shape[0] - rows, LANES), B16)
    normed, inverse = normalize(r.tokens[...].astype(F32))
    r.xhat1[...] = normed
    r.inv1[...] = inverse
    r.sums[0] = jnp.zeros((16, LANES), F32)
    for copy in gains:
        copy.wait_recv()
    for t in range(n_shard):
        columns = slice(t * part, (t + 1) * part)
        r.gain1[:, columns] = r.all_gains[t, 0:1].astype(F32)
        r.gain2[:, columns] = r.all_gains[t, 1:2].astype(F32)

    def normalize_half(start):
        @pl.loop(0, half // tok)
        def _(i):
            rows = aligned(start + i * tok, tok)
            values, _ = normalize(r.toks[rows].astype(F32))
            r.h1[rows] = (values * r.gain1[...]).astype(B16)

    tokens.finish_near()
    normalize_half(near_start)
    qkv.relay(0)
    win.start_far()
    grads.start_far()
    grads.start_near()
    win.start_near()
    qkv.relay(1)
    tokens.relay_all()
    tokens.finish_far()
    normalize_half(far_start)
    qkv.finish()

    @pl.loop(0, 2)
    def _(i):
        rows = aligned(i * half, half)
        projected = dot(r.h1[rows], r.w_qkv[...])
        cosine, sine = r.cosine[rows], r.sine[rows]
        for j in range(3 * part // LANES + 1):
            size = min(LANES, 3 * part - j * LANES)
            tile = projected[:, j * LANES : j * LANES + size]
            if (j + 1) * LANES <= 2 * part:
                tile = tile * cosine + turned(tile) * sine
                if j * LANES < part:
                    tile = tile * query_scale(j, part, half)
            tile = tile.astype(B16)
            for k in range(size // HEAD_DIM):
                index = j * (LANES // HEAD_DIM) + k
                r.heads[index, rows] = tile[:, k * HEAD_DIM : (k + 1) * HEAD_DIM]

    @pl.loop(0, heads)
    def _(h):
        key, value = r.heads[heads + h], r.heads[2 * heads + h]
        for b in range(2):
            rows = pl.ds(b * half, half)
            scores = times_transposed(r.heads[h, rows], key)
            maxima = jnp.max(scores, axis=-1, keepdims=True)
            expo = jnp.exp(scores - maxima)
            total = jnp.sum(expo, axis=-1, keepdims=True)
            probs = (expo * (1.0 / total)).astype(B16)
            r.probs[h, rows] = probs
            r.att_heads[h, rows] = dot(probs, value).astype(B16)

    win.relay(0)
    for h in range(heads):
        r.att[:, h * HEAD_DIM : (h + 1) * HEAD_DIM] = r.att_heads[h]

    def reduce(name):
        return ReduceScatter(
            place, sems, r.parts[name], r.nears[name], r.outgoing[name], r.fars[name], tok, chunks
        )

    def project(start):
        rows = aligned(start, half)
        r.parts["att"][rows] = dot(r.att[rows], r.w_out[...]).astype(B16)

    mixed = reduce("att")
    project(far_start)
    mixed.start_far()
    project(near_start)
    mixed.start_near()
    grads.relay_all()
    win.relay(1)
    mixed.forward()
    resid = r.tokens[...].astype(F32) + mixed.result()
    r.resid[...] = resid
    normed, inverse = normalize(resid)
    r.xhat2[...] = normed
    r.inv2[...] = inverse
    scaled = (normed * r.gain2[...]).astype(B16)
    r.h2[own] = scaled
    second = AllGather(place, sems, r.h2.at[own], r.h2, tok, chunks)
    second.start_far()
    second.start_near()
    win.finish()
    grads.finish_near()
    grads.finish_far()

    def feed_forward(start):
        rows = aligned(start, half)
        upper = dot(r.h2[rows], r.w_in[...])
        inner, gate = upper[:, :hidden], upper[:, hidden:]
        value, slope = gelu_pair(inner)
        act = (value * gate).astype(B16)
        r.act[rows] = act
        grad_act = times_transposed(r.grads[rows], r.down[...])
        grad_upper = jnp.concatenate(
            [grad_act * gate * slope, grad_act * value], axis=-1
        ).astype(B16)
        r.gup[rows] = grad_upper
        r.parts["h2"][rows] = times_transposed(grad_upper, r.w_in[...]).astype(B16)
        r.parts["down"][rows] = dot(act, r.down[...]).astype(B16)

    back2, down = reduce("h2"), reduce("down")
    second.finish_near()
    feed_forward(near_start)
    back2.start_near()
    second.relay_all()
    second.finish_far()
    feed_forward(far_start)
    back2.start_far()
    down.start_near()
    down.start_far()

    groups = {}
    for name, streams, swap in cfg.groups:
        groups[name] = [
            RepSum(place, sems, stream, swap, r.acc[name], r.box[name], r.res[name])
            for stream in streams
        ]
    active = []

    def launch(name):
        for item in groups[name]:
            item.begin()
            active.append(item)

    def pump():
        for item in active:
            if not item.done():
                item.advance()

    pack_rows(outer_sum(r.act[...], r.grads[...]), r.acc["down"])
    launch("down")
    back2.forward()

    def pack_pairs(left, right, target):
        for i in range(n_shard // 2):
            columns = slice(i * 2 * part, (i + 1) * 2 * part)
            values = outer_sum(left[:, columns], right[...])
            pack_block(values[:part], target, 2 * i)
            pack_block(values[part:], target, 2 * i + 1)

    pack_pairs(r.h2, r.gup, r.acc["in"])
    launch("in")
    grad_h2 = back2.result()
    back, gain_grad = norm_backward(grad_h2, r.xhat2[...], r.inv2[...], r.gain2[...])
    for j in range(width // LANES):
        r.sums[0, 8 + j : 9 + j] = gain_grad[:, j * LANES : (j + 1) * LANES]
    grad_resid = r.grad[...].astype(F32) + back
    r.gres[...] = grad_resid
    r.resid_b[own] = grad_resid.astype(B16)
    third = AllGather(place, sems, r.resid_b.at[own], r.resid_b, tok, chunks)
    third.start_far()
    third.start_near()
    down.forward()
    pump()

    def attention_grad(start):
        rows = aligned(start, half)
        values = times_transposed(r.resid_b[rows], r.w_out[...]).astype(B16)
        for h in range(heads):
            r.gatt[h, rows] = values[:, h * HEAD_DIM : (h + 1) * HEAD_DIM]

    third.finish_near()
    attention_grad(near_start)
    third.relay_all()
    third.finish_far()
    attention_grad(far_start)
    pack_rows(outer_sum(r.att[...], r.resid_b[...]), r.acc["out"])
    launch("out")

    for h in range(heads):
        key, value, query = r.heads[heads + h], r.heads[2 * heads + h], r.heads[h]
        grad_value = jnp.zeros((count, HEAD_DIM), F32)
        grad_key = jnp.zeros((count, HEAD_DIM), F32)
        for b in range(2):
            rows = pl.ds(b * half, half)
            grad_head = r.gatt[h, rows]
            probs = r.probs[h, rows]
            attended = r.att_heads[h, rows].astype(F32)
            delta = jnp.sum(grad_head.astype(F32) * attended, axis=-1, keepdims=True)
            grad_value = grad_value + outer_sum(probs, grad_head)
            grad_probs = times_transposed(grad_head, value)
            grad_scores = (probs.astype(F32) * (grad_probs - delta)).astype(B16)
            r.gheads[h, rows] = dot(grad_scores, key)
            grad_key = grad_key + outer_sum(grad_scores, query[b * half : (b + 1) * half])
        r.gheads[heads + h] = grad_key
        r.gheads[2 * heads + h] = grad_value
        if h == cfg.pump_head:
            pump()

    pump()
    grad_parts = reduce("h1")

    def project_back(start):
        rows = aligned(start, half)
        cosine, sine = r.cosine[rows], r.sine[rows]
        for j in range(3 * part // LANES + 1):
            size = min(LANES, 3 * part - j * LANES)
            index = j * (LANES // HEAD_DIM)
            tile = jnp.concatenate(
                [r.gheads[index + k, rows] for k in range(size // HEAD_DIM)], axis=-1
            )
            if (j + 1) * LANES <= 2 * part:
                tile = tile * cosine - turned(tile) * sine
                if j * LANES < part:
                    tile = tile * query_scale(j, part, half)
            r.gproj[rows, j * LANES : j * LANES + size] = tile.astype(B16)
        r.parts["h1"][rows] = times_transposed(r.gproj[rows], r.w_qkv[...]).astype(B16)

    project_back(far_start)
    grad_parts.start_far()
    project_back(near_start)
    grad_parts.start_near()
    pack_pairs(r.h1, r.gproj, r.acc["qkv"])
    launch("qkv")
    grad_parts.forward()
    r.o_output[...] = (r.resid[...] + down.result()).astype(B16)
    pump()
    grad_h1 = grad_parts.result()
    back, gain_grad = norm_backward(grad_h1, r.xhat1[...], r.inv1[...], r.gain1[...])
    for j in range(width // LANES):
        r.sums[0, j : j + 1] = gain_grad[:, j * LANES : (j + 1) * LANES]
    small = Total(
        place, sems, r.sums, r.boxes,
        [("shard", 1), ("shard", 2)] + [("rep", bit) for bit in rep_bits],
    )
    small.begin()
    active.append(small)
    r.o_tokens[...] = r.gres[...] + back
    while not all(item.done() for item in active):
        pump()
    r.o_total[...] = r.sums[len(small.bits)]
    for copy in gains:
        copy.wait_send()
    for item in [qkv, win, tokens, grads, second, third, mixed, back2, down, grad_parts]:
        item.close()
    for item in active:
        item.close()


def finish_kernel(cfg, *refs):
    ins, outs = refs[:7], refs[7:15]
    stage_qkv, stage_out, stage_in, stage_down, sems = refs[15:]
    output, grad_tokens, total, res_down, res_in, res_out, res_qkv = ins
    o_output, o_tokens, o_gain1, o_qkv, o_out, o_gain2, o_in, o_down = outs
    copies = []

    def send(source, target, pieces):
        size = source.shape[0] // pieces
        for i in range(pieces):
            rows = pl.ds(i * size, size)
            copy = pltpu.make_async_copy(source.at[rows], target.at[rows], sems.at[len(copies)])
            copy.start()
            copies.append(copy)

    send(output, o_output, 1)
    send(grad_tokens, o_tokens, 1)
    for t in range(cfg.n_shard):
        unpack_block(res_qkv, stage_qkv, t, 3)
    send(stage_qkv, o_qkv, 4)
    for t in range(cfg.n_shard):
        unpack_block(res_in, stage_in, t, 2)
    send(stage_in, o_in, 4)
    unpack_rows(res_down, stage_down)
    send(stage_down, o_down, 2)
    unpack_rows(res_out, stage_out)
    send(stage_out, o_out, 2)
    me = lax.axis_index("shard")
    for out, at in ((o_gain1, 0), (o_gain2, 8)):
        row = jnp.concatenate(
            [total[at + j : at + j + 1] for j in range(cfg.width // LANES)], axis=1
        )
        picked = jnp.zeros((1, cfg.part), F32)
        for t in range(cfg.n_shard):
            picked = jnp.where(me == t, row[:, t * cfg.part : (t + 1) * cfg.part], picked)
        out[...] = picked
    for copy in copies:
        copy.wait()


def rotary_tables(count):
    half = HEAD_DIM // 2
    freq = THETA ** (-np.arange(half, dtype=np.float64) * 2.0 / HEAD_DIM)
    angles = np.arange(count, dtype=np.float64)[:, None] * freq[None, :]
    angles = np.concatenate([angles, angles], axis=-1)
    sign = np.where(np.arange(HEAD_DIM) < half, -1.0, 1.0)
    repeat = LANES // HEAD_DIM
    cosine = np.tile(np.cos(angles), (1, repeat))
    sine = np.tile(np.sin(angles) * sign, (1, repeat))
    return cosine.astype(np.float32), sine.astype(np.float32)


def local(
    n_shard, n_rep, tokens, gain_one, qkv_weight, out_weight, gain_two, in_weight, down_weight,
    grad_output
):
    tok, width = tokens.shape[1:]
    cfg = Config()
    cfg.n_shard, cfg.n_rep, cfg.tok, cfg.width = n_shard, n_rep, tok, width
    cfg.part = part = width // n_shard
    cfg.heads = heads = part // HEAD_DIM
    cfg.hidden = hidden = down_weight.shape[0]
    cfg.count = count = tok * n_shard
    cfg.chunks = 2
    cfg.pump_head = 1
    cfg.limit = 44 * 1024 * 1024
    cfg.finish_limit = 16 * 1024 * 1024
    cfg.relays = min(2, n_rep.bit_length() - 1)
    while cfg.relays and part % (16 << cfg.relays):
        cfg.relays -= 1
    cosine, sine = rotary_tables(count)
    ins = dict(
        tokens=tokens.reshape(tok, width),
        gain_one=gain_one,
        gain_two=gain_two,
        qkv=qkv_weight,
        w_out=out_weight,
        win=in_weight,
        down=down_weight,
        grad=grad_output.reshape(tok, width),
        cosine=jnp.asarray(cosine),
        sine=jnp.asarray(sine),
    )
    outs = dict(
        o_output=((tok, width), B16),
        o_tokens=((tok, width), F32),
        o_total=((16, LANES), F32),
    )
    results = dict(
        o_output=((tok, width), B16),
        o_tokens=((tok, width), F32),
        o_gain1=((1, part), F32),
        o_qkv=((part, 3 * width), F32),
        o_out=((part, width), F32),
        o_gain2=((1, part), F32),
        o_in=((part, 2 * hidden * n_shard), F32),
        o_down=((hidden, width), F32),
    )
    scratch = dict(
        toks=((count, width), B16),
        grads=((count, width), B16),
        gains=((2, part), B16),
        all_gains=((n_shard, 2, part), B16),
        gain1=((1, width), F32),
        gain2=((1, width), F32),
        pk_qkv=((n_shard, part, 3 * part), B16),
        w_qkv=((width, 3 * part), B16),
        pk_in=((n_shard, part, 2 * hidden), B16),
        w_in=((width, 2 * hidden), B16),
        h1=((count, width), B16),
        heads=((3 * heads, count, HEAD_DIM), B16),
        probs=((heads, count, count), B16),
        att_heads=((heads, count, HEAD_DIM), B16),
        att=((count, part), B16),
        h2=((count, width), B16),
        act=((count, hidden), B16),
        gup=((count, 2 * hidden), B16),
        resid=((tok, width), F32),
        xhat1=((tok, width), F32),
        inv1=((tok, 1), F32),
        xhat2=((tok, width), F32),
        inv2=((tok, 1), F32),
        gres=((tok, width), F32),
        resid_b=((count, width), B16),
        gatt=((heads, count, HEAD_DIM), B16),
        gheads=((3 * heads, count, HEAD_DIM), F32),
        gproj=((count, 3 * part), B16),
        sums=((n_rep.bit_length() + 2, 16, LANES), F32),
        boxes=((n_rep.bit_length() + 1, 16, LANES), F32),
    )
    exchanges = ("att", "h2", "down", "h1")
    scratch.update(
        parts={name: ((count, width), B16) for name in exchanges},
        nears={name: ((2, tok, width), B16) for name in exchanges},
        outgoing={name: ((tok, width), B16) for name in exchanges},
        fars={name: ((tok, width), B16) for name in exchanges},
    )
    cfg.groups, cfg.padding, padded = [], [], {}
    for name, rows, swap in (
        ("down", hidden * width // LANES, False),
        ("in", part * 2 * hidden // LANES, True),
        ("out", part * width // LANES, False),
        ("qkv", part * 3 * part // LANES, True),
    ):
        streams, tall = streams_of(rows, n_rep)
        cfg.groups.append((name, streams, swap))
        if tall > rows:
            cfg.padding.append((name, rows))
        padded[name] = ((n_shard, tall, LANES) if swap else (tall, LANES), B16)
    scratch.update(acc=padded, box=padded)
    plain = list(ins) + list(outs)
    outs.update(padded)

    def is_entry(item):
        return isinstance(item, tuple)

    spaces = jax.tree.map(lambda entry: pltpu.VMEM(*entry), scratch, is_leaf=is_entry)
    spaces["sems"] = pltpu.SemaphoreType.DMA((SEMAPHORES,))
    spaces, cfg.tree = jax.tree.flatten(spaces)
    cfg.names, cfg.sums = plain, list(padded)
    middle = pl.pallas_call(
        functools.partial(layer_kernel, cfg),
        out_shape=tuple(jax.ShapeDtypeStruct(*entry) for entry in outs.values()),
        in_specs=[VMEM] * len(ins),
        out_specs=tuple([VMEM] * len(outs)),
        scratch_shapes=spaces,
        compiler_params=pltpu.CompilerParams(
            collective_id=0, has_side_effects=True, vmem_limit_bytes=cfg.limit
        ),
    )(*ins.values())
    anywhere = pl.BlockSpec(memory_space=pl.ANY)
    results = pl.pallas_call(
        functools.partial(finish_kernel, cfg),
        out_shape=tuple(jax.ShapeDtypeStruct(*entry) for entry in results.values()),
        in_specs=[VMEM] * len(middle),
        out_specs=tuple(VMEM if "gain" in name else anywhere for name in results),
        scratch_shapes=[
            pltpu.VMEM(*results[name]) for name in ("o_qkv", "o_out", "o_in", "o_down")
        ]
        + [pltpu.SemaphoreType.DMA((16,))],
        compiler_params=pltpu.CompilerParams(vmem_limit_bytes=cfg.finish_limit),
    )(*middle)
    output, grad_tokens, gain1, grad_qkv, grad_out, gain2, grad_in, grad_down = results
    return (
        output.reshape(1, tok, width),
        grad_tokens.reshape(1, tok, width),
        gain1.reshape(part),
        grad_qkv,
        grad_out,
        gain2.reshape(part),
        grad_in,
        grad_down,
    )


def solution(mesh):
    in_specs = (
        P("rep", "shard", None),
        P("shard"),
        P("shard", None),
        P("shard", None),
        P("shard"),
        P("shard", None),
        P("shard", None),
        P("rep", "shard", None),
    )
    out_specs = (
        P("rep", "shard", None),
        P("rep", "shard", None),
        P("shard"),
        P("shard", None),
        P("shard", None),
        P("shard"),
        P("shard", None),
        P("shard", None),
    )
    body = functools.partial(local, mesh.shape["shard"], mesh.shape["rep"])
    return jax.shard_map(body, mesh=mesh, in_specs=in_specs, out_specs=out_specs, check_vma=False)
```

```python
import functools

import jax
import jax.numpy as jnp
import numpy as np
from jax import lax
from jax.experimental import pallas as pl
from jax.experimental.pallas import tpu as pltpu
from jax.sharding import PartitionSpec as P

HEAD_DIM = 64
EPSILON = 1e-05
THETA = 160000.0
SQRT_HALF = 0.7071067811865476
INV_SQRT_TAU = 0.3989422804014327
MESH_ID = pl.DeviceIdType.MESH
LANES = 128
VMEM = pl.BlockSpec(memory_space=pltpu.VMEM)
F32 = jnp.float32
B16 = jnp.bfloat16
SEMAPHORES = 448


def normalize(values):
    mean_row = jnp.mean(values, axis=-1, keepdims=True)
    centred = values - mean_row
    variance = jnp.mean(centred * centred, axis=-1, keepdims=True)
    inverse = lax.rsqrt(variance + EPSILON)
    return (centred * inverse, inverse)


def norm_backward(grad_out, normed, inverse, gain):
    grad_normed = grad_out * gain
    gain_grad = jnp.sum(grad_out * normed, axis=0, keepdims=True)
    first = jnp.mean(grad_normed, axis=-1, keepdims=True)
    second = jnp.mean(grad_normed * normed, axis=-1, keepdims=True)
    return (inverse * (grad_normed - first - normed * second), gain_grad)


def gelu_pair(inner):
    cdf = 0.5 * (1.0 + lax.erf(inner * SQRT_HALF))
    return (inner * cdf, cdf + inner * jnp.exp(-0.5 * inner * inner) * INV_SQRT_TAU)


def dot(left, right):
    return jnp.dot(left, right, preferred_element_type=F32)


def outer_sum(left, right):
    return lax.dot_general(left, right, (((0,), (0,)), ((), ())), preferred_element_type=F32)


def times_transposed(left, right):
    return lax.dot_general(left, right, (((1,), (1,)), ((), ())), preferred_element_type=F32)


def flip(index, bit):
    return index + bit * (1 - 2 * ((index // bit) % 2))


def aligned(start, size, unit=16):
    if not isinstance(start, int):
        start = pl.multiple_of(start, unit)
    return pl.ds(start, size)


def remote(src, dst, sems, axis, target):
    return pltpu.make_async_remote_copy(
        src_ref=src,
        dst_ref=dst,
        send_sem=sems(),
        recv_sem=sems(),
        device_id={axis: target},
        device_id_type=MESH_ID,
    )


class Pool:
    def __init__(self, ref):
        self.ref, self.used = ref, 0

    def __call__(self):
        self.used += 1
        assert self.used <= SEMAPHORES
        return self.ref.at[self.used - 1]


class Place:
    def __init__(self):
        self.me = lax.axis_index("shard")
        self.rep = lax.axis_index("rep")
        self.core = flip(self.me, 1)
        self.chip = flip(self.me, 2)
        self.diagonal = flip(self.core, 2)


class AllGather:
    def __init__(self, place, sems, src, dst, tok, chunks):
        self.far, self.near, self.relays = [], [], []
        self.place, self.sems, self.dst, self.tok, self.chunks = place, sems, dst, tok, chunks
        size = tok // chunks
        for c in range(chunks):
            part = src.at[pl.ds(c * size, size)]
            self.far.append(remote(part, self.rows(place.me, c), sems, "shard", place.chip))
        for c in range(chunks):
            part = src.at[pl.ds(c * size, size)]
            self.near.append(remote(part, self.rows(place.me, c), sems, "shard", place.core))

    def rows(self, block, c):
        size = self.tok // self.chunks
        return self.dst.at[aligned(block * self.tok + c * size, size)]

    def start_far(self):
        for copy in self.far:
            copy.start()

    def start_near(self):
        for copy in self.near:
            copy.start()

    def relay(self, c):
        self.far[c].wait_recv()
        region = self.rows(self.place.chip, c)
        copy = remote(region, region, self.sems, "shard", self.place.core)
        copy.start()
        self.relays.append(copy)

    def relay_all(self):
        for c in range(self.chunks):
            self.relay(c)

    def finish_near(self):
        for copy in self.near:
            copy.wait_recv()

    def finish_far(self):
        for copy in self.relays:
            copy.wait_recv()

    def close(self):
        for copy in self.far + self.near + self.relays:
            copy.wait_send()


class ReduceScatter:
    def __init__(self, place, sems, part, near, outgoing, far, tok, chunks):
        self.place, self.sems, self.part, self.near = place, sems, part, near
        self.outgoing, self.far, self.tok, self.chunks = outgoing, far, tok, chunks
        self.size = tok // chunks
        self.first, self.second, self.third = [], [], []

    def rows(self, block, c):
        return aligned(block * self.tok + c * self.size, self.size)

    def piece(self, c):
        return pl.ds(c * self.size, self.size)

    def start(self, block, slot, copies):
        for c in range(self.chunks):
            copy = remote(
                self.part.at[self.rows(block, c)],
                self.near.at[slot, self.piece(c)],
                self.sems,
                "shard",
                self.place.core,
            )
            copy.start()
            copies.append(copy)

    def start_far(self):
        self.start(self.place.diagonal, 0, self.first)

    def start_near(self):
        self.start(self.place.core, 1, self.second)

    def forward(self):
        for c in range(self.chunks):
            self.first[c].wait_recv()
            piece = self.piece(c)
            mine = self.part[self.rows(self.place.chip, c)].astype(F32)
            self.outgoing[piece] = (mine + self.near[0, piece].astype(F32)).astype(B16)
            copy = remote(
                self.outgoing.at[piece], self.far.at[piece], self.sems, "shard", self.place.chip
            )
            copy.start()
            self.third.append(copy)

    def result(self):
        for copy in self.second + self.third:
            copy.wait_recv()
        mine = self.part[aligned(self.place.me * self.tok, self.tok)].astype(F32)
        return mine + self.near[1].astype(F32) + self.far[...].astype(F32)

    def close(self):
        for copy in self.first + self.second + self.third:
            copy.wait_send()


class Swap:
    def __init__(self, place, sems, source, packed, dest, kinds, relays):
        self.place, self.sems, self.source = place, sems, source
        self.packed, self.dest, self.kinds, self.relays = packed, dest, kinds, relays
        self.tall = source.shape[0]
        self.share = self.tall >> relays
        columns = dest.shape[1]
        cut = columns // LANES // 2 * LANES
        low = tuple(1 << i for i in range(relays))
        self.parts = []
        for first, size, order in ((0, cut, low), (cut, columns - cut, low[::-1])):
            position = 0
            for level, bit in enumerate(order):
                position = position + ((place.rep // bit) % 2) * (1 << level)
            self.parts.append((pl.ds(first, size), order, position))
        self.shared, self.whole = [], []

    def pack(self):
        blocks, _, columns = self.packed.shape
        size = columns // self.kinds
        for j in range(blocks):
            for kind in range(self.kinds):
                start = (kind * blocks + j) * size
                self.packed[j, :, kind * size : (kind + 1) * size] = self.source[
                    :, start : start + size
                ]

    def start_far(self):
        place = self.place
        for columns, order, position in self.parts:
            first = position * self.share
            for target in (place.chip, place.diagonal):
                copy = remote(
                    self.packed.at[target, aligned(first, self.share), columns],
                    self.dest.at[aligned(place.me * self.tall + first, self.share), columns],
                    self.sems,
                    "shard",
                    target,
                )
                copy.start()
                self.shared.append((target, columns, order, position, [copy]))

    def start_near(self):
        place = self.place
        mine = aligned(place.me * self.tall, self.tall)
        copy = remote(
            self.packed.at[place.core], self.dest.at[mine], self.sems, "shard", place.core
        )
        copy.start()
        self.whole.append(copy)
        self.dest[mine] = self.packed[place.me]

    def relay(self, level):
        if level >= self.relays:
            return
        for target, columns, order, position, copies in self.shared:
            copies[-1].wait_recv()
            length = self.share << level
            first = (position // (1 << level)) * length
            region = self.dest.at[aligned(target * self.tall + first, length), columns]
            copy = remote(region, region, self.sems, "rep", flip(self.place.rep, order[level]))
            copy.start()
            copies.append(copy)

    def finish(self):
        for entry in self.shared:
            entry[-1][-1].wait_recv()
        for copy in self.whole:
            copy.wait_recv()

    def close(self):
        for copy in self.whole:
            copy.wait_send()
        for entry in self.shared:
            for copy in entry[-1]:
                copy.wait_send()


def halves(order, index):
    length = 1 << len(order)
    offset = 0
    plan = []
    for bit in order:
        length //= 2
        side = (index // bit) % 2
        plan.append((bit, offset + side * length, offset + (1 - side) * length, length))
        offset = offset + side * length
    return plan


def streams_of(rows, n_rep):
    tiles = -(-rows // (16 * n_rep))
    low_first = tuple(1 << i for i in range(n_rep.bit_length() - 1))
    second = low_first[1::-1] + low_first[2:]
    third = low_first[:1] + low_first[2:] + low_first[1:2]
    quarter = tiles // 4
    shares = ((tiles // 2, second), (tiles - tiles // 2 - quarter, low_first), (quarter, third))
    streams = []
    base = 0
    for share, order in shares:
        if share:
            streams.append((base, 16 * share, order))
            base += 16 * share * n_rep
    return streams, base


class RepSum:
    def __init__(self, place, sems, stream, swap, acc, box, res):
        self.place, self.sems, self.swap = place, sems, swap
        self.base, self.rows, order = stream
        self.acc, self.box, self.res = acc, box, res
        self.steps = len(order)
        self.plan = halves(order, place.rep)
        self.started = []
        self.round = 0

    def at(self, ref, piece, length, lead=None):
        span = aligned(self.base + piece * self.rows, length * self.rows)
        if not self.swap:
            return ref.at[span]
        return ref.at[slice(None) if lead is None else lead, span]

    def begin(self):
        k, plan, steps, place, sems = self.round, self.plan, self.steps, self.place, self.sems
        acc, box, res = self.acc, self.box, self.res
        if k < steps:
            bit, _, sent, length = plan[k]
            source, target = self.at(acc, sent, length), self.at(box, length, length)
            copies = [remote(source, target, sems, "rep", flip(place.rep, bit))]
        elif k == steps:
            mine = plan[-1][1]
            if not self.swap:
                copies = [
                    pltpu.make_async_copy(self.at(acc, mine, 1), self.at(res, mine, 1), sems())
                ]
            else:
                target_block = self.at(res, mine, 1, place.me)
                copies = [
                    remote(self.at(acc, mine, 1, target), target_block, sems, "shard", target)
                    for target in (place.core, place.chip, place.diagonal)
                ]
                copies.append(
                    pltpu.make_async_copy(self.at(acc, mine, 1, place.me), target_block, sems())
                )
        else:
            bit, kept, _, length = plan[2 * steps - k]
            region = self.at(res, kept, length)
            copies = [remote(region, region, sems, "rep", flip(place.rep, bit))]
        for copy in copies:
            copy.start()
        self.started.append(copies)

    def finish(self):
        k = self.round
        copies = self.started[k]
        if k == self.steps:
            for copy in copies:
                copy.wait()
            return
        copies[0].wait_recv()
        if k > self.steps:
            return
        acc, box, base, rows = self.acc, self.box, self.base, self.rows
        _, kept, _, length = self.plan[k]
        blocks = range(acc.shape[0]) if self.swap else (None,)

        @pl.loop(0, length)
        def _(p):
            to = aligned(base + (kept + p) * rows, rows)
            of = aligned(base + (length + p) * rows, rows)
            for block in blocks:
                x, y = ((to,), (of,)) if block is None else ((block, to), (block, of))
                acc[x] = (acc[x].astype(F32) + box[y].astype(F32)).astype(B16)

    def advance(self):
        self.finish()
        self.round += 1
        if not self.done():
            self.begin()

    def done(self):
        return self.round > 2 * self.steps

    def close(self):
        for k in range(2 * self.steps + 1):
            if k != self.steps:
                self.started[k][0].wait_send()


class Total:
    def __init__(self, place, sems, sums, boxes, bits):
        self.place, self.sems, self.sums, self.boxes, self.bits = place, sems, sums, boxes, bits
        self.copies = []
        self.round = 0

    def begin(self):
        level = len(self.copies)
        axis, bit = self.bits[level]
        index = self.place.me if axis == "shard" else self.place.rep
        copy = remote(
            self.sums.at[level], self.boxes.at[level], self.sems, axis, flip(index, bit)
        )
        copy.start()
        self.copies.append(copy)

    def advance(self):
        level = len(self.copies) - 1
        if level >= len(self.bits):
            return
        self.copies[level].wait_recv()
        self.sums[level + 1] = self.sums[level] + self.boxes[level]
        if level + 1 < len(self.bits):
            self.begin()
        else:
            self.copies.append(None)

    def done(self):
        return len(self.copies) > len(self.bits)

    def close(self):
        for copy in self.copies[:-1]:
            copy.wait_send()


def pack_block(values, target, t):
    rows, columns = values.shape
    full, rest = divmod(columns, LANES)
    values = values.astype(B16)
    for j in range(full):
        target[t, j * rows : (j + 1) * rows] = values[:, j * LANES : (j + 1) * LANES]
    if rest:
        half = rows // 2
        tail = values[:, full * LANES :]
        target[t, full * rows : full * rows + half] = jnp.concatenate(
            [tail[:half], tail[half:]], axis=1
        )


def unpack_block(source, out, t, kinds):
    blocks = source.shape[0]
    rows, width = out.shape
    columns = width // blocks
    size = columns // kinds
    full, rest = divmod(columns, LANES)
    parts = [source[t, j * rows : (j + 1) * rows] for j in range(full)]
    if rest:
        tail = source[t, full * rows : full * rows + rows // 2]
        parts.append(jnp.concatenate([tail[:, :rest], tail[:, rest:]], axis=0))
    block = jnp.concatenate(parts, axis=1).astype(F32)
    for kind in range(kinds):
        start = (kind * blocks + t) * size
        out[:, start : start + size] = block[:, kind * size : (kind + 1) * size]


def pack_rows(values, target):
    rows = values.shape[0]
    values = values.astype(B16)
    for j in range(values.shape[1] // LANES):
        target[j * rows : (j + 1) * rows] = values[:, j * LANES : (j + 1) * LANES]


def unpack_rows(source, out):
    rows = out.shape[0]
    for j in range(out.shape[1] // LANES):
        out[:, j * LANES : (j + 1) * LANES] = source[j * rows : (j + 1) * rows].astype(F32)


def turned(values):
    lane = lax.broadcasted_iota(jnp.int32, values.shape, 1)
    half = HEAD_DIM // 2
    ahead = pltpu.roll(values, LANES - half, 1)
    behind = pltpu.roll(values, half, 1)
    return jnp.where(lane % HEAD_DIM < half, ahead, behind)


def query_scale(tile, part, rows):
    lane = lax.broadcasted_iota(jnp.int32, (rows, LANES), 1) + tile * LANES
    return jnp.where(lane < part, HEAD_DIM ** (-0.5), 1.0)


class Config:
    pass


def layer_kernel(cfg, *refs):
    r = Config()
    arguments = dict(zip(cfg.inputs, refs))
    refs = refs[len(cfg.inputs) :]
    r.__dict__.update(zip(cfg.names, refs))
    refs = refs[len(cfg.names) :]
    r.res = dict(zip(cfg.sums, refs))
    r.__dict__.update(jax.tree.unflatten(cfg.tree, refs[len(cfg.sums) :]))
    tok, width, part, heads, hidden = cfg.tok, cfg.width, cfg.part, cfg.heads, cfg.hidden
    n_shard, count, chunks = cfg.n_shard, cfg.count, cfg.chunks
    place = Place()
    sems = Pool(r.sems)
    me, core, chip, diagonal = place.me, place.core, place.chip, place.diagonal
    rep_bits = [1 << b for b in range(cfg.n_rep.bit_length() - 1)]
    partners = [("shard", core), ("shard", chip), ("shard", diagonal)]
    partners += [("rep", flip(place.rep, bit)) for bit in rep_bits]
    barrier = pltpu.get_barrier_semaphore()
    for axis, target in partners:
        pl.semaphore_signal(barrier, inc=1, device_id={axis: target}, device_id_type=MESH_ID)
    loads = {}
    for name in cfg.inputs:
        loads[name] = pltpu.make_async_copy(arguments[name], getattr(r, name), sems())
        loads[name].start()
    own = aligned(me * tok, tok)
    half = count // 2
    near_start = (me // 2) * half
    far_start = (chip // 2) * half

    qkv = Swap(place, sems, r.qkv, r.pk_qkv, r.w_qkv, 3, cfg.relays)
    win = Swap(place, sems, r.win, r.pk_in, r.w_in, 2, cfg.relays)
    tokens = AllGather(place, sems, r.tokens, r.toks, tok, chunks)
    grads = AllGather(place, sems, r.grad, r.grads, tok, chunks)
    gains = [
        remote(r.gains, r.all_gains.at[me], sems, "shard", target)
        for target in (core, chip, diagonal)
    ]
    loads["gain_one"].wait()
    loads["gain_two"].wait()
    r.gains[0:1] = r.gain_one[...].reshape(1, part)
    r.gains[1:2] = r.gain_two[...].reshape(1, part)
    loads["qkv"].wait()
    qkv.pack()
    for name in ("tokens", "win", "grad"):
        loads[name].wait()
    pl.semaphore_wait(barrier, len(partners))
    for copy in gains:
        copy.start()
    qkv.start_far()
    tokens.start_far()
    tokens.start_near()
    qkv.start_near()
    r.toks[own] = r.tokens[...]
    r.grads[own] = r.grad[...]
    r.all_gains[me] = r.gains[...]
    win.pack()
    for name, rows in cfg.padding:
        acc = r.acc[name]
        if len(acc.shape) == 3:
            acc[:, rows:] = jnp.zeros((n_shard, acc.shape[1] - rows, LANES), B16)
        else:
            acc[rows:] = jnp.zeros((acc.shape[0] - rows, LANES), B16)
    normed, inverse = normalize(r.tokens[...].astype(F32))
    r.xhat1[...] = normed
    r.inv1[...] = inverse
    r.sums[0] = jnp.zeros((16, LANES), F32)
    for copy in gains:
        copy.wait_recv()
    for t in range(n_shard):
        columns = slice(t * part, (t + 1) * part)
        r.gain1[:, columns] = r.all_gains[t, 0:1].astype(F32)
        r.gain2[:, columns] = r.all_gains[t, 1:2].astype(F32)

    def normalize_half(start):
        @pl.loop(0, half // tok)
        def _(i):
            rows = aligned(start + i * tok, tok)
            values, _ = normalize(r.toks[rows].astype(F32))
            r.h1[rows] = (values * r.gain1[...]).astype(B16)

    tokens.finish_near()
    normalize_half(near_start)
    qkv.relay(0)
    win.start_far()
    grads.start_far()
    grads.start_near()
    win.start_near()
    qkv.relay(1)
    tokens.relay_all()
    tokens.finish_far()
    normalize_half(far_start)
    qkv.finish()

    loads["cosine"].wait()
    loads["sine"].wait()
    @pl.loop(0, 2)
    def _(i):
        rows = aligned(i * half, half)
        projected = dot(r.h1[rows], r.w_qkv[...])
        cosine, sine = r.cosine[rows], r.sine[rows]
        for j in range(3 * part // LANES + 1):
            size = min(LANES, 3 * part - j * LANES)
            tile = projected[:, j * LANES : j * LANES + size]
            if (j + 1) * LANES <= 2 * part:
                tile = tile * cosine + turned(tile) * sine
                if j * LANES < part:
                    tile = tile * query_scale(j, part, half)
            tile = tile.astype(B16)
            for k in range(size // HEAD_DIM):
                index = j * (LANES // HEAD_DIM) + k
                r.heads[index, rows] = tile[:, k * HEAD_DIM : (k + 1) * HEAD_DIM]

    @pl.loop(0, heads)
    def _(h):
        key, value = r.heads[heads + h], r.heads[2 * heads + h]
        for b in range(2):
            rows = pl.ds(b * half, half)
            scores = times_transposed(r.heads[h, rows], key)
            maxima = jnp.max(scores, axis=-1, keepdims=True)
            expo = jnp.exp(scores - maxima)
            total = jnp.sum(expo, axis=-1, keepdims=True)
            probs = (expo * (1.0 / total)).astype(B16)
            r.probs[h, rows] = probs
            r.att_heads[h, rows] = dot(probs, value).astype(B16)

    win.relay(0)
    for h in range(heads):
        r.att[:, h * HEAD_DIM : (h + 1) * HEAD_DIM] = r.att_heads[h]

    def reduce(name):
        return ReduceScatter(
            place, sems, r.parts[name], r.nears[name], r.outgoing[name], r.fars[name], tok, chunks
        )

    def project(start):
        rows = aligned(start, half)
        r.parts["att"][rows] = dot(r.att[rows], r.w_out[...]).astype(B16)

    mixed = reduce("att")
    loads["w_out"].wait()
    loads["down"].wait()
    project(far_start)
    mixed.start_far()
    project(near_start)
    mixed.start_near()
    mixed.forward()
    win.relay(1)
    grads.relay_all()
    resid = r.tokens[...].astype(F32) + mixed.result()
    r.resid[...] = resid
    normed, inverse = normalize(resid)
    r.xhat2[...] = normed
    r.inv2[...] = inverse
    scaled = (normed * r.gain2[...]).astype(B16)
    r.h2[own] = scaled
    second = AllGather(place, sems, r.h2.at[own], r.h2, tok, chunks)
    second.start_far()
    second.start_near()
    win.finish()
    grads.finish_near()
    grads.finish_far()

    def feed_forward(start):
        rows = aligned(start, half)
        upper = dot(r.h2[rows], r.w_in[...])
        inner, gate = upper[:, :hidden], upper[:, hidden:]
        value, slope = gelu_pair(inner)
        act = (value * gate).astype(B16)
        r.act[rows] = act
        grad_act = times_transposed(r.grads[rows], r.down[...])
        grad_upper = jnp.concatenate(
            [grad_act * gate * slope, grad_act * value], axis=-1
        ).astype(B16)
        r.gup[rows] = grad_upper
        r.parts["h2"][rows] = times_transposed(grad_upper, r.w_in[...]).astype(B16)
        r.parts["down"][rows] = dot(act, r.down[...]).astype(B16)

    back2, down = reduce("h2"), reduce("down")
    second.finish_near()
    feed_forward(near_start)
    back2.start_near()
    second.relay_all()
    second.finish_far()
    feed_forward(far_start)
    back2.start_far()
    down.start_near()
    down.start_far()

    groups = {}
    for name, streams, swap in cfg.groups:
        groups[name] = [
            RepSum(place, sems, stream, swap, r.acc[name], r.box[name], r.res[name])
            for stream in streams
        ]
    active = []

    def launch(name):
        for item in groups[name]:
            item.begin()
            active.append(item)

    def pump(items=None, least=0):
        for item in active if items is None else items:
            if item.round >= least and not item.done():
                item.advance()

    pack_rows(outer_sum(r.act[...], r.grads[...]), r.acc["down"])
    launch("down")
    back2.forward()

    def pack_pairs(left, right, target):
        for i in range(n_shard // 2):
            columns = slice(i * 2 * part, (i + 1) * 2 * part)
            values = outer_sum(left[:, columns], right[...])
            pack_block(values[:part], target, 2 * i)
            pack_block(values[part:], target, 2 * i + 1)

    pack_pairs(r.h2, r.gup, r.acc["in"])
    launch("in")
    grad_h2 = back2.result()
    pump(groups["down"])
    back, gain_grad = norm_backward(grad_h2, r.xhat2[...], r.inv2[...], r.gain2[...])
    for j in range(width // LANES):
        r.sums[0, 8 + j : 9 + j] = gain_grad[:, j * LANES : (j + 1) * LANES]
    grad_resid = r.grad[...].astype(F32) + back
    r.gres[...] = grad_resid
    r.resid_b[own] = grad_resid.astype(B16)
    third = AllGather(place, sems, r.resid_b.at[own], r.resid_b, tok, chunks)
    third.start_far()
    third.start_near()
    down.forward()

    def attention_grad(start):
        rows = aligned(start, half)
        values = times_transposed(r.resid_b[rows], r.w_out[...]).astype(B16)
        for h in range(heads):
            r.gatt[h, rows] = values[:, h * HEAD_DIM : (h + 1) * HEAD_DIM]

    third.finish_near()
    attention_grad(near_start)
    third.relay_all()
    pump()
    third.finish_far()
    attention_grad(far_start)
    pack_rows(outer_sum(r.att[...], r.resid_b[...]), r.acc["out"])
    launch("out")

    for h in range(heads):
        key, value, query = r.heads[heads + h], r.heads[2 * heads + h], r.heads[h]
        grad_value = jnp.zeros((count, HEAD_DIM), F32)
        grad_key = jnp.zeros((count, HEAD_DIM), F32)
        for b in range(2):
            rows = pl.ds(b * half, half)
            grad_head = r.gatt[h, rows]
            probs = r.probs[h, rows]
            attended = r.att_heads[h, rows].astype(F32)
            delta = jnp.sum(grad_head.astype(F32) * attended, axis=-1, keepdims=True)
            grad_value = grad_value + outer_sum(probs, grad_head)
            grad_probs = times_transposed(grad_head, value)
            grad_scores = (probs.astype(F32) * (grad_probs - delta)).astype(B16)
            r.gheads[h, rows] = dot(grad_scores, key)
            grad_key = grad_key + outer_sum(grad_scores, query[b * half : (b + 1) * half])
        r.gheads[heads + h] = grad_key
        r.gheads[2 * heads + h] = grad_value
        if h < cfg.pump_heads:
            pump()

    grad_parts = reduce("h1")

    def project_back(start):
        rows = aligned(start, half)
        cosine, sine = r.cosine[rows], r.sine[rows]
        for j in range(3 * part // LANES + 1):
            size = min(LANES, 3 * part - j * LANES)
            index = j * (LANES // HEAD_DIM)
            tile = jnp.concatenate(
                [r.gheads[index + k, rows] for k in range(size // HEAD_DIM)], axis=-1
            )
            if (j + 1) * LANES <= 2 * part:
                tile = tile * cosine - turned(tile) * sine
                if j * LANES < part:
                    tile = tile * query_scale(j, part, half)
            r.gproj[rows, j * LANES : j * LANES + size] = tile.astype(B16)
        r.parts["h1"][rows] = times_transposed(r.gproj[rows], r.w_qkv[...]).astype(B16)

    project_back(far_start)
    grad_parts.start_far()
    project_back(near_start)
    grad_parts.start_near()
    pack_pairs(r.h1, r.gproj, r.acc["qkv"])
    launch("qkv")
    grad_parts.forward()
    r.o_output[...] = (r.resid[...] + down.result()).astype(B16)
    pump(None, 1)
    grad_h1 = grad_parts.result()
    back, gain_grad = norm_backward(grad_h1, r.xhat1[...], r.inv1[...], r.gain1[...])
    for j in range(width // LANES):
        r.sums[0, j : j + 1] = gain_grad[:, j * LANES : (j + 1) * LANES]
    small = Total(
        place, sems, r.sums, r.boxes,
        [("shard", 1), ("shard", 2)] + [("rep", bit) for bit in rep_bits],
    )
    small.begin()
    active.append(small)
    r.o_tokens[...] = r.gres[...] + back
    while not all(item.done() for item in active):
        pump()
    r.o_total[...] = r.sums[len(small.bits)]
    for copy in gains:
        copy.wait_send()
    for item in [qkv, win, tokens, grads, second, third, mixed, back2, down, grad_parts]:
        item.close()
    for item in active:
        item.close()


def finish_kernel(cfg, *refs):
    ins, outs = refs[:7], refs[7:15]
    stage_qkv, stage_out, stage_in, stage_down, sems = refs[15:]
    output, grad_tokens, total, res_down, res_in, res_out, res_qkv = ins
    o_output, o_tokens, o_gain1, o_qkv, o_out, o_gain2, o_in, o_down = outs
    copies = []

    def send(source, target, pieces):
        size = source.shape[0] // pieces
        for i in range(pieces):
            rows = pl.ds(i * size, size)
            copy = pltpu.make_async_copy(source.at[rows], target.at[rows], sems.at[len(copies)])
            copy.start()
            copies.append(copy)

    send(output, o_output, 1)
    send(grad_tokens, o_tokens, 1)
    for t in range(cfg.n_shard):
        unpack_block(res_qkv, stage_qkv, t, 3)
    send(stage_qkv, o_qkv, 4)
    for t in range(cfg.n_shard):
        unpack_block(res_in, stage_in, t, 2)
    send(stage_in, o_in, 4)
    unpack_rows(res_down, stage_down)
    send(stage_down, o_down, 2)
    unpack_rows(res_out, stage_out)
    send(stage_out, o_out, 2)
    me = lax.axis_index("shard")
    for out, at in ((o_gain1, 0), (o_gain2, 8)):
        row = jnp.concatenate(
            [total[at + j : at + j + 1] for j in range(cfg.width // LANES)], axis=1
        )
        picked = jnp.zeros((1, cfg.part), F32)
        for t in range(cfg.n_shard):
            picked = jnp.where(me == t, row[:, t * cfg.part : (t + 1) * cfg.part], picked)
        out[...] = picked
    for copy in copies:
        copy.wait()


def rotary_tables(count):
    half = HEAD_DIM // 2
    freq = THETA ** (-np.arange(half, dtype=np.float64) * 2.0 / HEAD_DIM)
    angles = np.arange(count, dtype=np.float64)[:, None] * freq[None, :]
    angles = np.concatenate([angles, angles], axis=-1)
    sign = np.where(np.arange(HEAD_DIM) < half, -1.0, 1.0)
    repeat = LANES // HEAD_DIM
    cosine = np.tile(np.cos(angles), (1, repeat))
    sine = np.tile(np.sin(angles) * sign, (1, repeat))
    return cosine.astype(np.float32), sine.astype(np.float32)


def local(
    n_shard, n_rep, tokens, gain_one, qkv_weight, out_weight, gain_two, in_weight, down_weight,
    grad_output
):
    tok, width = tokens.shape[1:]
    cfg = Config()
    cfg.n_shard, cfg.n_rep, cfg.tok, cfg.width = n_shard, n_rep, tok, width
    cfg.part = part = width // n_shard
    cfg.heads = heads = part // HEAD_DIM
    cfg.hidden = hidden = down_weight.shape[0]
    cfg.count = count = tok * n_shard
    cfg.chunks = 2
    cfg.pump_heads = 2
    cfg.limit = 44 * 1024 * 1024
    cfg.finish_limit = 16 * 1024 * 1024
    cfg.relays = min(2, n_rep.bit_length() - 1)
    while cfg.relays and part % (16 << cfg.relays):
        cfg.relays -= 1
    cosine, sine = rotary_tables(count)
    ins = dict(
        gain_one=gain_one,
        gain_two=gain_two,
        qkv=qkv_weight,
        tokens=tokens.reshape(tok, width),
        win=in_weight,
        grad=grad_output.reshape(tok, width),
        cosine=jnp.asarray(cosine),
        sine=jnp.asarray(sine),
        w_out=out_weight,
        down=down_weight,
    )
    outs = dict(
        o_output=((tok, width), B16),
        o_tokens=((tok, width), F32),
        o_total=((16, LANES), F32),
    )
    results = dict(
        o_output=((tok, width), B16),
        o_tokens=((tok, width), F32),
        o_gain1=((1, part), F32),
        o_qkv=((part, 3 * width), F32),
        o_out=((part, width), F32),
        o_gain2=((1, part), F32),
        o_in=((part, 2 * hidden * n_shard), F32),
        o_down=((hidden, width), F32),
    )
    scratch = dict(
        toks=((count, width), B16),
        grads=((count, width), B16),
        gains=((2, part), B16),
        all_gains=((n_shard, 2, part), B16),
        gain1=((1, width), F32),
        gain2=((1, width), F32),
        pk_qkv=((n_shard, part, 3 * part), B16),
        w_qkv=((width, 3 * part), B16),
        pk_in=((n_shard, part, 2 * hidden), B16),
        w_in=((width, 2 * hidden), B16),
        h1=((count, width), B16),
        heads=((3 * heads, count, HEAD_DIM), B16),
        probs=((heads, count, count), B16),
        att_heads=((heads, count, HEAD_DIM), B16),
        att=((count, part), B16),
        h2=((count, width), B16),
        act=((count, hidden), B16),
        gup=((count, 2 * hidden), B16),
        resid=((tok, width), F32),
        xhat1=((tok, width), F32),
        inv1=((tok, 1), F32),
        xhat2=((tok, width), F32),
        inv2=((tok, 1), F32),
        gres=((tok, width), F32),
        resid_b=((count, width), B16),
        gatt=((heads, count, HEAD_DIM), B16),
        gheads=((3 * heads, count, HEAD_DIM), F32),
        gproj=((count, 3 * part), B16),
        sums=((n_rep.bit_length() + 2, 16, LANES), F32),
        boxes=((n_rep.bit_length() + 1, 16, LANES), F32),
    )
    exchanges = ("att", "h2", "down", "h1")
    scratch.update(
        parts={name: ((count, width), B16) for name in exchanges},
        nears={name: ((2, tok, width), B16) for name in exchanges},
        outgoing={name: ((tok, width), B16) for name in exchanges},
        fars={name: ((tok, width), B16) for name in exchanges},
    )
    cfg.groups, cfg.padding, padded = [], [], {}
    for name, rows, swap in (
        ("down", hidden * width // LANES, False),
        ("in", part * 2 * hidden // LANES, True),
        ("out", part * width // LANES, False),
        ("qkv", part * 3 * part // LANES, True),
    ):
        streams, tall = streams_of(rows, n_rep)
        cfg.groups.append((name, streams, swap))
        if tall > rows:
            cfg.padding.append((name, rows))
        padded[name] = ((n_shard, tall, LANES) if swap else (tall, LANES), B16)
    scratch.update(acc=padded, box=padded)
    scratch.update({name: (value.shape, value.dtype) for name, value in ins.items()})
    plain = list(outs)
    outs.update(padded)

    def is_entry(item):
        return isinstance(item, tuple)

    spaces = jax.tree.map(lambda entry: pltpu.VMEM(*entry), scratch, is_leaf=is_entry)
    spaces["sems"] = pltpu.SemaphoreType.DMA((SEMAPHORES,))
    spaces, cfg.tree = jax.tree.flatten(spaces)
    cfg.inputs, cfg.names, cfg.sums = list(ins), plain, list(padded)
    middle = pl.pallas_call(
        functools.partial(layer_kernel, cfg),
        out_shape=tuple(jax.ShapeDtypeStruct(*entry) for entry in outs.values()),
        in_specs=[pl.BlockSpec(memory_space=pltpu.HBM)] * len(ins),
        out_specs=tuple([VMEM] * len(outs)),
        scratch_shapes=spaces,
        compiler_params=pltpu.CompilerParams(
            collective_id=0, has_side_effects=True, vmem_limit_bytes=cfg.limit
        ),
    )(*[pltpu.with_memory_space_constraint(value, pltpu.HBM) for value in ins.values()])
    anywhere = pl.BlockSpec(memory_space=pl.ANY)
    results = pl.pallas_call(
        functools.partial(finish_kernel, cfg),
        out_shape=tuple(jax.ShapeDtypeStruct(*entry) for entry in results.values()),
        in_specs=[VMEM] * len(middle),
        out_specs=tuple(VMEM if "gain" in name else anywhere for name in results),
        scratch_shapes=[
            pltpu.VMEM(*results[name]) for name in ("o_qkv", "o_out", "o_in", "o_down")
        ]
        + [pltpu.SemaphoreType.DMA((16,))],
        compiler_params=pltpu.CompilerParams(vmem_limit_bytes=cfg.finish_limit),
    )(*middle)
    output, grad_tokens, gain1, grad_qkv, grad_out, gain2, grad_in, grad_down = results
    return (
        output.reshape(1, tok, width),
        grad_tokens.reshape(1, tok, width),
        gain1.reshape(part),
        grad_qkv,
        grad_out,
        gain2.reshape(part),
        grad_in,
        grad_down,
    )


def solution(mesh):
    in_specs = (
        P("rep", "shard", None),
        P("shard"),
        P("shard", None),
        P("shard", None),
        P("shard"),
        P("shard", None),
        P("shard", None),
        P("rep", "shard", None),
    )
    out_specs = (
        P("rep", "shard", None),
        P("rep", "shard", None),
        P("shard"),
        P("shard", None),
        P("shard", None),
        P("shard"),
        P("shard", None),
        P("shard", None),
    )
    body = functools.partial(local, mesh.shape["shard"], mesh.shape["rep"])
    return jax.shard_map(body, mesh=mesh, in_specs=in_specs, out_specs=out_specs, check_vma=False)
```

```python
import functools
import heapq

import jax
import jax.numpy as jnp
import numpy as np
from jax import lax
from jax.experimental import pallas as pl
from jax.experimental.pallas import tpu as pltpu
from jax.sharding import PartitionSpec as P

HEAD_DIM = 64
EPSILON = 1e-05
THETA = 160000.0
SQRT_HALF = 0.7071067811865476
INV_SQRT_TAU = 0.3989422804014327
MESH_ID = pl.DeviceIdType.MESH
LANES = 128
VMEM = pl.BlockSpec(memory_space=pltpu.VMEM)
F32 = jnp.float32
B16 = jnp.bfloat16
SEMAPHORES = 576
HOP_US = 1.9
LINK_BYTES_PER_US = 90000.0


def normalize(values):
    mean_row = jnp.mean(values, axis=-1, keepdims=True)
    centred = values - mean_row
    variance = jnp.mean(centred * centred, axis=-1, keepdims=True)
    inverse = lax.rsqrt(variance + EPSILON)
    return (centred * inverse, inverse)


def norm_backward(grad_out, normed, inverse, gain):
    grad_normed = grad_out * gain
    gain_grad = jnp.sum(grad_out * normed, axis=0, keepdims=True)
    first = jnp.mean(grad_normed, axis=-1, keepdims=True)
    second = jnp.mean(grad_normed * normed, axis=-1, keepdims=True)
    return (inverse * (grad_normed - first - normed * second), gain_grad)


def gelu_pair(inner):
    cdf = 0.5 * (1.0 + lax.erf(inner * SQRT_HALF))
    return (inner * cdf, cdf + inner * jnp.exp(-0.5 * inner * inner) * INV_SQRT_TAU)


def dot(left, right):
    return jnp.dot(left, right, preferred_element_type=F32)


def outer_sum(left, right):
    return lax.dot_general(left, right, (((0,), (0,)), ((), ())), preferred_element_type=F32)


def times_transposed(left, right):
    return lax.dot_general(left, right, (((1,), (1,)), ((), ())), preferred_element_type=F32)


def flip(index, bit):
    return index + bit * (1 - 2 * ((index // bit) % 2))


def aligned(start, size, unit=16):
    if not isinstance(start, int):
        start = pl.multiple_of(start, unit)
    return pl.ds(start, size)


def remote(src, dst, sems, axis, target):
    return pltpu.make_async_remote_copy(
        src_ref=src,
        dst_ref=dst,
        send_sem=sems(),
        recv_sem=sems(),
        device_id={axis: target},
        device_id_type=MESH_ID,
    )


class Pool:
    def __init__(self, ref):
        self.ref, self.used = ref, 0

    def __call__(self):
        self.used += 1
        assert self.used <= SEMAPHORES
        return self.ref.at[self.used - 1]


class Place:
    def __init__(self):
        self.me = lax.axis_index("shard")
        self.rep = lax.axis_index("rep")
        self.core = flip(self.me, 1)
        self.chip = flip(self.me, 2)
        self.diagonal = flip(self.core, 2)


class AllGather:
    def __init__(self, place, sems, src, dst, tok, chunks):
        self.far, self.near, self.relays = [], [], []
        self.place, self.sems, self.dst, self.tok, self.chunks = place, sems, dst, tok, chunks
        size = tok // chunks
        for c in range(chunks):
            part = src.at[pl.ds(c * size, size)]
            self.far.append(remote(part, self.rows(place.me, c), sems, "shard", place.chip))
        for c in range(chunks):
            part = src.at[pl.ds(c * size, size)]
            self.near.append(remote(part, self.rows(place.me, c), sems, "shard", place.core))

    def rows(self, block, c):
        size = self.tok // self.chunks
        return self.dst.at[aligned(block * self.tok + c * size, size)]

    def start_far(self):
        for copy in self.far:
            copy.start()

    def start_near(self):
        for copy in self.near:
            copy.start()

    def relay(self, c):
        self.far[c].wait_recv()
        region = self.rows(self.place.chip, c)
        copy = remote(region, region, self.sems, "shard", self.place.core)
        copy.start()
        self.relays.append(copy)

    def relay_all(self):
        for c in range(self.chunks):
            self.relay(c)

    def finish_near(self):
        for copy in self.near:
            copy.wait_recv()

    def finish_far(self):
        for copy in self.relays:
            copy.wait_recv()

    def close(self):
        for copy in self.far + self.near + self.relays:
            copy.wait_send()


class ReduceScatter:
    def __init__(self, place, sems, part, near, outgoing, far, tok, chunks):
        self.place, self.sems, self.part, self.near = place, sems, part, near
        self.outgoing, self.far, self.tok, self.chunks = outgoing, far, tok, chunks
        self.size = tok // chunks
        self.first, self.second, self.third = [], [], []

    def rows(self, block, c):
        return aligned(block * self.tok + c * self.size, self.size)

    def piece(self, c):
        return pl.ds(c * self.size, self.size)

    def start(self, block, slot, copies):
        for c in range(self.chunks):
            copy = remote(
                self.part.at[self.rows(block, c)],
                self.near.at[slot, self.piece(c)],
                self.sems,
                "shard",
                self.place.core,
            )
            copy.start()
            copies.append(copy)

    def start_far(self):
        self.start(self.place.diagonal, 0, self.first)

    def start_near(self):
        self.start(self.place.core, 1, self.second)

    def forward(self):
        for c in range(self.chunks):
            self.first[c].wait_recv()
            piece = self.piece(c)
            mine = self.part[self.rows(self.place.chip, c)].astype(F32)
            self.outgoing[piece] = (mine + self.near[0, piece].astype(F32)).astype(B16)
            copy = remote(
                self.outgoing.at[piece], self.far.at[piece], self.sems, "shard", self.place.chip
            )
            copy.start()
            self.third.append(copy)

    def result(self):
        for copy in self.second + self.third:
            copy.wait_recv()
        mine = self.part[aligned(self.place.me * self.tok, self.tok)].astype(F32)
        return mine + self.near[1].astype(F32) + self.far[...].astype(F32)

    def close(self):
        for copy in self.first + self.second + self.third:
            copy.wait_send()


class Swap:
    def __init__(self, place, sems, source, packed, dest, kinds, relays):
        self.place, self.sems, self.source = place, sems, source
        self.packed, self.dest, self.kinds, self.relays = packed, dest, kinds, relays
        self.tall = source.shape[0]
        self.share = self.tall >> relays
        columns = dest.shape[1]
        cut = columns // LANES // 2 * LANES
        low = tuple(1 << i for i in range(relays))
        self.parts = []
        for first, size, order in ((0, cut, low), (cut, columns - cut, low[::-1])):
            position = 0
            for level, bit in enumerate(order):
                position = position + ((place.rep // bit) % 2) * (1 << level)
            self.parts.append((pl.ds(first, size), order, position))
        self.shared, self.whole = [], []

    def pack(self):
        blocks, _, columns = self.packed.shape
        size = columns // self.kinds
        for j in range(blocks):
            for kind in range(self.kinds):
                start = (kind * blocks + j) * size
                self.packed[j, :, kind * size : (kind + 1) * size] = self.source[
                    :, start : start + size
                ]

    def start_far(self):
        place = self.place
        for columns, order, position in self.parts:
            first = position * self.share
            for target in (place.chip, place.diagonal):
                copy = remote(
                    self.packed.at[target, aligned(first, self.share), columns],
                    self.dest.at[aligned(place.me * self.tall + first, self.share), columns],
                    self.sems,
                    "shard",
                    target,
                )
                copy.start()
                self.shared.append((target, columns, order, position, [copy]))

    def start_near(self):
        place = self.place
        mine = aligned(place.me * self.tall, self.tall)
        copy = remote(
            self.packed.at[place.core], self.dest.at[mine], self.sems, "shard", place.core
        )
        copy.start()
        self.whole.append(copy)
        self.dest[mine] = self.packed[place.me]

    def relay(self, level):
        if level >= self.relays:
            return
        for target, columns, order, position, copies in self.shared:
            copies[-1].wait_recv()
            length = self.share << level
            first = (position // (1 << level)) * length
            region = self.dest.at[aligned(target * self.tall + first, length), columns]
            copy = remote(region, region, self.sems, "rep", flip(self.place.rep, order[level]))
            copy.start()
            copies.append(copy)

    def finish(self):
        for entry in self.shared:
            entry[-1][-1].wait_recv()
        for copy in self.whole:
            copy.wait_recv()

    def close(self):
        for copy in self.whole:
            copy.wait_send()
        for entry in self.shared:
            for copy in entry[-1]:
                copy.wait_send()


def halves(order, index):
    length = 1 << len(order)
    offset = 0
    plan = []
    for bit in order:
        length //= 2
        side = (index // bit) % 2
        plan.append((bit, offset + side * length, offset + (1 - side) * length, length))
        offset = offset + side * length
    return plan


def streams_of(rows, n_rep, most):
    tiles = -(-rows // (16 * n_rep))
    low_first = tuple(1 << i for i in range(n_rep.bit_length() - 1))
    second = low_first[1::-1] + low_first[2:]
    most = min(most, tiles)
    streams = []
    base = 0
    for i in range(most):
        share = tiles // most + (i < tiles % most)
        streams.append((base, 16 * share, second if i % 3 == 1 else low_first))
        base += 16 * share * n_rep
    return streams, base


class Schedule:
    def __init__(self):
        self.free = {}
        self.queue = []
        self.count = 0

    def put(self, item, now):
        for link, time in item.cost():
            start = max(now, self.free.get(link, 0.0))
            self.free[link] = start + time
        self.count += 1
        heapq.heappush(self.queue, (start + time + HOP_US, self.count, item))

    def launch(self, items, now):
        for item in items:
            item.begin()
            self.put(item, now)

    def pump(self, now, until=None):
        until = now if until is None else until
        while self.queue and self.queue[0][0] <= until:
            arrival, _, item = heapq.heappop(self.queue)
            item.advance()
            if not item.done():
                self.put(item, max(arrival, now))


class RepSum:
    def __init__(self, place, sems, stream, swap, acc, box, res):
        self.place, self.sems, self.swap = place, sems, swap
        self.base, self.rows, order = stream
        self.acc, self.box, self.res = acc, box, res
        self.steps = len(order)
        self.plan = halves(order, place.rep)
        self.started = []
        self.round = 0

    def at(self, ref, piece, length, lead=None):
        span = aligned(self.base + piece * self.rows, length * self.rows)
        if not self.swap:
            return ref.at[span]
        return ref.at[slice(None) if lead is None else lead, span]

    def begin(self):
        k, plan, steps, place, sems = self.round, self.plan, self.steps, self.place, self.sems
        acc, box, res = self.acc, self.box, self.res
        if k < steps:
            bit, _, sent, length = plan[k]
            source, target = self.at(acc, sent, length), self.at(box, length, length)
            copies = [remote(source, target, sems, "rep", flip(place.rep, bit))]
        elif k == steps:
            mine = plan[-1][1]
            if not self.swap:
                copies = [
                    pltpu.make_async_copy(self.at(acc, mine, 1), self.at(res, mine, 1), sems())
                ]
            else:
                target_block = self.at(res, mine, 1, place.me)
                copies = [
                    remote(self.at(acc, mine, 1, target), target_block, sems, "shard", target)
                    for target in (place.core, place.chip, place.diagonal)
                ]
                copies.append(
                    pltpu.make_async_copy(self.at(acc, mine, 1, place.me), target_block, sems())
                )
        else:
            bit, kept, _, length = plan[2 * steps - k]
            region = self.at(res, kept, length)
            copies = [remote(region, region, sems, "rep", flip(place.rep, bit))]
        for copy in copies:
            copy.start()
        self.started.append(copies)

    def finish(self):
        k = self.round
        copies = self.started[k]
        if k == self.steps:
            for copy in copies:
                copy.wait()
            return
        copies[0].wait_recv()
        if k > self.steps:
            return
        acc, box, base, rows = self.acc, self.box, self.base, self.rows
        _, kept, _, length = self.plan[k]
        blocks = range(acc.shape[0]) if self.swap else (None,)

        @pl.loop(0, length)
        def _(p):
            to = aligned(base + (kept + p) * rows, rows)
            of = aligned(base + (length + p) * rows, rows)
            for block in blocks:
                x, y = ((to,), (of,)) if block is None else ((block, to), (block, of))
                acc[x] = (acc[x].astype(F32) + box[y].astype(F32)).astype(B16)

    def advance(self):
        self.finish()
        self.round += 1
        if not self.done():
            self.begin()

    def done(self):
        return self.round > 2 * self.steps

    def cost(self):
        k, steps = self.round, self.steps
        blocks = self.acc.shape[0] if self.swap else 1
        piece = 2 * self.rows * LANES * 2 * blocks / LINK_BYTES_PER_US
        if k == steps:
            return [(-1, piece / 2 if self.swap else 0.0)]
        bit, _, _, length = self.plan[k if k < steps else 2 * steps - k]
        if bit > 2:
            return [(2, piece * length), (bit, 2 * piece * length)]
        return [(bit, piece * length)]

    def close(self):
        for k in range(2 * self.steps + 1):
            if k != self.steps:
                self.started[k][0].wait_send()


class Total:
    def __init__(self, place, sems, sums, boxes, bits):
        self.place, self.sems, self.sums, self.boxes, self.bits = place, sems, sums, boxes, bits
        self.copies = []
        self.round = 0

    def begin(self):
        level = len(self.copies)
        axis, bit = self.bits[level]
        index = self.place.me if axis == "shard" else self.place.rep
        copy = remote(
            self.sums.at[level], self.boxes.at[level], self.sems, axis, flip(index, bit)
        )
        copy.start()
        self.copies.append(copy)

    def advance(self):
        level = len(self.copies) - 1
        if level >= len(self.bits):
            return
        self.copies[level].wait_recv()
        self.sums[level + 1] = self.sums[level] + self.boxes[level]
        if level + 1 < len(self.bits):
            self.begin()
        else:
            self.copies.append(None)

    def done(self):
        return len(self.copies) > len(self.bits)

    def cost(self):
        return [(0, 0.0)]

    def close(self):
        for copy in self.copies[:-1]:
            copy.wait_send()


def pack_block(values, target, t):
    rows, columns = values.shape
    full, rest = divmod(columns, LANES)
    values = values.astype(B16)
    for j in range(full):
        target[t, j * rows : (j + 1) * rows] = values[:, j * LANES : (j + 1) * LANES]
    if rest:
        half = rows // 2
        tail = values[:, full * LANES :]
        target[t, full * rows : full * rows + half] = jnp.concatenate(
            [tail[:half], tail[half:]], axis=1
        )


def unpack_block(source, out, t, kinds):
    blocks = source.shape[0]
    rows, width = out.shape
    columns = width // blocks
    size = columns // kinds
    full, rest = divmod(columns, LANES)
    parts = [source[t, j * rows : (j + 1) * rows] for j in range(full)]
    if rest:
        tail = source[t, full * rows : full * rows + rows // 2]
        parts.append(jnp.concatenate([tail[:, :rest], tail[:, rest:]], axis=0))
    block = jnp.concatenate(parts, axis=1).astype(F32)
    for kind in range(kinds):
        start = (kind * blocks + t) * size
        out[:, start : start + size] = block[:, kind * size : (kind + 1) * size]


def pack_rows(values, target):
    rows = values.shape[0]
    values = values.astype(B16)
    for j in range(values.shape[1] // LANES):
        target[j * rows : (j + 1) * rows] = values[:, j * LANES : (j + 1) * LANES]


def unpack_rows(source, out):
    rows = out.shape[0]
    for j in range(out.shape[1] // LANES):
        out[:, j * LANES : (j + 1) * LANES] = source[j * rows : (j + 1) * rows].astype(F32)


def turned(values):
    lane = lax.broadcasted_iota(jnp.int32, values.shape, 1)
    half = HEAD_DIM // 2
    ahead = pltpu.roll(values, LANES - half, 1)
    behind = pltpu.roll(values, half, 1)
    return jnp.where(lane % HEAD_DIM < half, ahead, behind)


def query_scale(tile, part, rows):
    lane = lax.broadcasted_iota(jnp.int32, (rows, LANES), 1) + tile * LANES
    return jnp.where(lane < part, HEAD_DIM ** (-0.5), 1.0)


class Config:
    pass


def layer_kernel(cfg, *refs):
    r = Config()
    arguments = dict(zip(cfg.inputs, refs))
    refs = refs[len(cfg.inputs) :]
    r.__dict__.update(zip(cfg.names, refs))
    refs = refs[len(cfg.names) :]
    r.res = dict(zip(cfg.sums, refs))
    r.__dict__.update(jax.tree.unflatten(cfg.tree, refs[len(cfg.sums) :]))
    tok, width, part, heads, hidden = cfg.tok, cfg.width, cfg.part, cfg.heads, cfg.hidden
    n_shard, count, chunks = cfg.n_shard, cfg.count, cfg.chunks
    place = Place()
    sems = Pool(r.sems)
    me, core, chip, diagonal = place.me, place.core, place.chip, place.diagonal
    rep_bits = [1 << b for b in range(cfg.n_rep.bit_length() - 1)]
    partners = [("shard", core), ("shard", chip), ("shard", diagonal)]
    partners += [("rep", flip(place.rep, bit)) for bit in rep_bits]
    barrier = pltpu.get_barrier_semaphore()
    for axis, target in partners:
        pl.semaphore_signal(barrier, inc=1, device_id={axis: target}, device_id_type=MESH_ID)
    loads = {}
    for name in cfg.inputs:
        loads[name] = pltpu.make_async_copy(arguments[name], getattr(r, name), sems())
        loads[name].start()
    own = aligned(me * tok, tok)
    half = count // 2
    near_start = (me // 2) * half
    far_start = (chip // 2) * half

    qkv = Swap(place, sems, r.qkv, r.pk_qkv, r.w_qkv, 3, cfg.relays)
    win = Swap(place, sems, r.win, r.pk_in, r.w_in, 2, cfg.relays)
    tokens = AllGather(place, sems, r.tokens, r.toks, tok, chunks)
    grads = AllGather(place, sems, r.grad, r.grads, tok, chunks)
    gains = [
        remote(r.gains, r.all_gains.at[me], sems, "shard", target)
        for target in (core, chip, diagonal)
    ]
    loads["gain_one"].wait()
    loads["gain_two"].wait()
    r.gains[0:1] = r.gain_one[...].reshape(1, part)
    r.gains[1:2] = r.gain_two[...].reshape(1, part)
    loads["qkv"].wait()
    qkv.pack()
    for name in ("tokens", "win", "grad"):
        loads[name].wait()
    pl.semaphore_wait(barrier, len(partners))
    for copy in gains:
        copy.start()
    qkv.start_far()
    tokens.start_far()
    tokens.start_near()
    qkv.start_near()
    r.toks[own] = r.tokens[...]
    r.grads[own] = r.grad[...]
    r.all_gains[me] = r.gains[...]
    win.pack()
    for name, rows in cfg.padding:
        acc = r.acc[name]
        if len(acc.shape) == 3:
            acc[:, rows:] = jnp.zeros((n_shard, acc.shape[1] - rows, LANES), B16)
        else:
            acc[rows:] = jnp.zeros((acc.shape[0] - rows, LANES), B16)
    normed, inverse = normalize(r.tokens[...].astype(F32))
    r.xhat1[...] = normed
    r.inv1[...] = inverse
    r.sums[0] = jnp.zeros((16, LANES), F32)
    for copy in gains:
        copy.wait_recv()
    for t in range(n_shard):
        columns = slice(t * part, (t + 1) * part)
        r.gain1[:, columns] = r.all_gains[t, 0:1].astype(F32)
        r.gain2[:, columns] = r.all_gains[t, 1:2].astype(F32)

    def normalize_half(start):
        @pl.loop(0, half // tok)
        def _(i):
            rows = aligned(start + i * tok, tok)
            values, _ = normalize(r.toks[rows].astype(F32))
            r.h1[rows] = (values * r.gain1[...]).astype(B16)

    tokens.finish_near()
    normalize_half(near_start)
    qkv.relay(0)
    win.start_far()
    grads.start_far()
    grads.start_near()
    win.start_near()
    qkv.relay(1)
    tokens.relay_all()
    tokens.finish_far()
    normalize_half(far_start)
    qkv.finish()

    loads["cosine"].wait()
    loads["sine"].wait()
    @pl.loop(0, 2)
    def _(i):
        rows = aligned(i * half, half)
        projected = dot(r.h1[rows], r.w_qkv[...])
        cosine, sine = r.cosine[rows], r.sine[rows]
        for j in range(3 * part // LANES + 1):
            size = min(LANES, 3 * part - j * LANES)
            tile = projected[:, j * LANES : j * LANES + size]
            if (j + 1) * LANES <= 2 * part:
                tile = tile * cosine + turned(tile) * sine
                if j * LANES < part:
                    tile = tile * query_scale(j, part, half)
            tile = tile.astype(B16)
            for k in range(size // HEAD_DIM):
                index = j * (LANES // HEAD_DIM) + k
                r.heads[index, rows] = tile[:, k * HEAD_DIM : (k + 1) * HEAD_DIM]

    @pl.loop(0, heads)
    def _(h):
        key, value = r.heads[heads + h], r.heads[2 * heads + h]
        for b in range(2):
            rows = pl.ds(b * half, half)
            scores = times_transposed(r.heads[h, rows], key)
            maxima = jnp.max(scores, axis=-1, keepdims=True)
            expo = jnp.exp(scores - maxima)
            total = jnp.sum(expo, axis=-1, keepdims=True)
            probs = (expo * (1.0 / total)).astype(B16)
            r.probs[h, rows] = probs
            r.att_heads[h, rows] = dot(probs, value).astype(B16)

    win.relay(0)
    for h in range(heads):
        r.att[:, h * HEAD_DIM : (h + 1) * HEAD_DIM] = r.att_heads[h]

    def reduce(name):
        return ReduceScatter(
            place, sems, r.parts[name], r.nears[name], r.outgoing[name], r.fars[name], tok, chunks
        )

    def project(start):
        rows = aligned(start, half)
        r.parts["att"][rows] = dot(r.att[rows], r.w_out[...]).astype(B16)

    mixed = reduce("att")
    loads["w_out"].wait()
    loads["down"].wait()
    project(far_start)
    mixed.start_far()
    project(near_start)
    mixed.start_near()
    mixed.forward()
    win.relay(1)
    grads.relay_all()
    resid = r.tokens[...].astype(F32) + mixed.result()
    r.resid[...] = resid
    normed, inverse = normalize(resid)
    r.xhat2[...] = normed
    r.inv2[...] = inverse
    scaled = (normed * r.gain2[...]).astype(B16)
    r.h2[own] = scaled
    second = AllGather(place, sems, r.h2.at[own], r.h2, tok, chunks)
    second.start_far()
    second.start_near()
    win.finish()
    grads.finish_near()
    grads.finish_far()

    def feed_forward(start):
        rows = aligned(start, half)
        upper = dot(r.h2[rows], r.w_in[...])
        inner, gate = upper[:, :hidden], upper[:, hidden:]
        value, slope = gelu_pair(inner)
        act = (value * gate).astype(B16)
        r.act[rows] = act
        grad_act = times_transposed(r.grads[rows], r.down[...])
        grad_upper = jnp.concatenate(
            [grad_act * gate * slope, grad_act * value], axis=-1
        ).astype(B16)
        r.gup[rows] = grad_upper
        r.parts["h2"][rows] = times_transposed(grad_upper, r.w_in[...]).astype(B16)
        r.parts["down"][rows] = dot(act, r.down[...]).astype(B16)

    back2, down = reduce("h2"), reduce("down")
    second.finish_near()
    feed_forward(near_start)
    back2.start_near()
    second.relay_all()
    second.finish_far()
    feed_forward(far_start)
    back2.start_far()
    down.start_near()
    down.start_far()

    groups = {}
    for name, streams, swap in cfg.groups:
        groups[name] = [
            RepSum(place, sems, stream, swap, r.acc[name], r.box[name], r.res[name])
            for stream in streams
        ]
    plan = Schedule()

    pack_rows(outer_sum(r.act[...], r.grads[...]), r.acc["down"])
    plan.launch(groups["down"], 0.0)
    back2.forward()

    def pack_pairs(left, right, target):
        for i in range(n_shard // 2):
            columns = slice(i * 2 * part, (i + 1) * 2 * part)
            values = outer_sum(left[:, columns], right[...])
            pack_block(values[:part], target, 2 * i)
            pack_block(values[part:], target, 2 * i + 1)

    pack_pairs(r.h2, r.gup, r.acc["in"])
    plan.launch(groups["in"], 1.6)
    plan.pump(1.6, 5.6)
    grad_h2 = back2.result()
    back, gain_grad = norm_backward(grad_h2, r.xhat2[...], r.inv2[...], r.gain2[...])
    for j in range(width // LANES):
        r.sums[0, 8 + j : 9 + j] = gain_grad[:, j * LANES : (j + 1) * LANES]
    grad_resid = r.grad[...].astype(F32) + back
    r.gres[...] = grad_resid
    r.resid_b[own] = grad_resid.astype(B16)
    third = AllGather(place, sems, r.resid_b.at[own], r.resid_b, tok, chunks)
    third.start_far()
    third.start_near()
    down.forward()
    plan.pump(7.0)

    def attention_grad(start):
        rows = aligned(start, half)
        values = times_transposed(r.resid_b[rows], r.w_out[...]).astype(B16)
        for h in range(heads):
            r.gatt[h, rows] = values[:, h * HEAD_DIM : (h + 1) * HEAD_DIM]

    third.finish_near()
    attention_grad(near_start)
    plan.pump(8.5, 9.5)
    third.relay(0)
    plan.pump(10.5, 11.5)
    third.relay(1)
    plan.pump(12.0)
    third.finish_far()
    attention_grad(far_start)
    pack_rows(outer_sum(r.att[...], r.resid_b[...]), r.acc["out"])
    plan.pump(13.5)
    plan.launch(groups["out"], 13.5)

    for h in range(heads):
        key, value, query = r.heads[heads + h], r.heads[2 * heads + h], r.heads[h]
        grad_value = jnp.zeros((count, HEAD_DIM), F32)
        grad_key = jnp.zeros((count, HEAD_DIM), F32)
        for b in range(2):
            rows = pl.ds(b * half, half)
            grad_head = r.gatt[h, rows]
            probs = r.probs[h, rows]
            attended = r.att_heads[h, rows].astype(F32)
            delta = jnp.sum(grad_head.astype(F32) * attended, axis=-1, keepdims=True)
            grad_value = grad_value + outer_sum(probs, grad_head)
            grad_probs = times_transposed(grad_head, value)
            grad_scores = (probs.astype(F32) * (grad_probs - delta)).astype(B16)
            r.gheads[h, rows] = dot(grad_scores, key)
            grad_key = grad_key + outer_sum(grad_scores, query[b * half : (b + 1) * half])
        r.gheads[heads + h] = grad_key
        r.gheads[2 * heads + h] = grad_value
        plan.pump(14.4 + 0.9 * h)

    grad_parts = reduce("h1")

    def project_back(start):
        rows = aligned(start, half)
        cosine, sine = r.cosine[rows], r.sine[rows]
        for j in range(3 * part // LANES + 1):
            size = min(LANES, 3 * part - j * LANES)
            index = j * (LANES // HEAD_DIM)
            tile = jnp.concatenate(
                [r.gheads[index + k, rows] for k in range(size // HEAD_DIM)], axis=-1
            )
            if (j + 1) * LANES <= 2 * part:
                tile = tile * cosine - turned(tile) * sine
                if j * LANES < part:
                    tile = tile * query_scale(j, part, half)
            r.gproj[rows, j * LANES : j * LANES + size] = tile.astype(B16)
        r.parts["h1"][rows] = times_transposed(r.gproj[rows], r.w_qkv[...]).astype(B16)

    project_back(far_start)
    grad_parts.start_far()
    project_back(near_start)
    grad_parts.start_near()
    plan.pump(17.9)
    pack_pairs(r.h1, r.gproj, r.acc["qkv"])
    plan.launch(groups["qkv"], 18.9)
    grad_parts.forward()
    r.o_output[...] = (r.resid[...] + down.result()).astype(B16)
    plan.pump(19.5, 24.0)
    grad_h1 = grad_parts.result()
    back, gain_grad = norm_backward(grad_h1, r.xhat1[...], r.inv1[...], r.gain1[...])
    for j in range(width // LANES):
        r.sums[0, j : j + 1] = gain_grad[:, j * LANES : (j + 1) * LANES]
    small = Total(
        place, sems, r.sums, r.boxes,
        [("shard", 1), ("shard", 2)] + [("rep", bit) for bit in rep_bits],
    )
    plan.launch([small], 25.0)
    r.o_tokens[...] = r.gres[...] + back
    plan.pump(25.5, float("inf"))
    r.o_total[...] = r.sums[len(small.bits)]
    for copy in gains:
        copy.wait_send()
    for item in [qkv, win, tokens, grads, second, third, mixed, back2, down, grad_parts]:
        item.close()
    for item in sum(groups.values(), [small]):
        item.close()


def finish_kernel(cfg, *refs):
    ins, outs = refs[:7], refs[7:15]
    stage_qkv, stage_out, stage_in, stage_down, sems = refs[15:]
    output, grad_tokens, total, res_down, res_in, res_out, res_qkv = ins
    o_output, o_tokens, o_gain1, o_qkv, o_out, o_gain2, o_in, o_down = outs
    copies = []

    def send(source, target, pieces):
        size = source.shape[0] // pieces
        for i in range(pieces):
            rows = pl.ds(i * size, size)
            copy = pltpu.make_async_copy(source.at[rows], target.at[rows], sems.at[len(copies)])
            copy.start()
            copies.append(copy)

    send(output, o_output, 1)
    send(grad_tokens, o_tokens, 1)
    for t in range(cfg.n_shard):
        unpack_block(res_qkv, stage_qkv, t, 3)
    send(stage_qkv, o_qkv, 4)
    for t in range(cfg.n_shard):
        unpack_block(res_in, stage_in, t, 2)
    send(stage_in, o_in, 4)
    unpack_rows(res_down, stage_down)
    send(stage_down, o_down, 2)
    unpack_rows(res_out, stage_out)
    send(stage_out, o_out, 2)
    me = lax.axis_index("shard")
    for out, at in ((o_gain1, 0), (o_gain2, 8)):
        row = jnp.concatenate(
            [total[at + j : at + j + 1] for j in range(cfg.width // LANES)], axis=1
        )
        picked = jnp.zeros((1, cfg.part), F32)
        for t in range(cfg.n_shard):
            picked = jnp.where(me == t, row[:, t * cfg.part : (t + 1) * cfg.part], picked)
        out[...] = picked
    for copy in copies:
        copy.wait()


def rotary_tables(count):
    half = HEAD_DIM // 2
    freq = THETA ** (-np.arange(half, dtype=np.float64) * 2.0 / HEAD_DIM)
    angles = np.arange(count, dtype=np.float64)[:, None] * freq[None, :]
    angles = np.concatenate([angles, angles], axis=-1)
    sign = np.where(np.arange(HEAD_DIM) < half, -1.0, 1.0)
    repeat = LANES // HEAD_DIM
    cosine = np.tile(np.cos(angles), (1, repeat))
    sine = np.tile(np.sin(angles) * sign, (1, repeat))
    return cosine.astype(np.float32), sine.astype(np.float32)


def local(
    n_shard, n_rep, tokens, gain_one, qkv_weight, out_weight, gain_two, in_weight, down_weight,
    grad_output
):
    tok, width = tokens.shape[1:]
    cfg = Config()
    cfg.n_shard, cfg.n_rep, cfg.tok, cfg.width = n_shard, n_rep, tok, width
    cfg.part = part = width // n_shard
    cfg.heads = heads = part // HEAD_DIM
    cfg.hidden = hidden = down_weight.shape[0]
    cfg.count = count = tok * n_shard
    cfg.chunks = 2
    cfg.limit = 44 * 1024 * 1024
    cfg.finish_limit = 16 * 1024 * 1024
    cfg.relays = min(2, n_rep.bit_length() - 1)
    while cfg.relays and part % (16 << cfg.relays):
        cfg.relays -= 1
    cosine, sine = rotary_tables(count)
    ins = dict(
        gain_one=gain_one,
        gain_two=gain_two,
        qkv=qkv_weight,
        tokens=tokens.reshape(tok, width),
        win=in_weight,
        grad=grad_output.reshape(tok, width),
        cosine=jnp.asarray(cosine),
        sine=jnp.asarray(sine),
        w_out=out_weight,
        down=down_weight,
    )
    outs = dict(
        o_output=((tok, width), B16),
        o_tokens=((tok, width), F32),
        o_total=((16, LANES), F32),
    )
    results = dict(
        o_output=((tok, width), B16),
        o_tokens=((tok, width), F32),
        o_gain1=((1, part), F32),
        o_qkv=((part, 3 * width), F32),
        o_out=((part, width), F32),
        o_gain2=((1, part), F32),
        o_in=((part, 2 * hidden * n_shard), F32),
        o_down=((hidden, width), F32),
    )
    scratch = dict(
        toks=((count, width), B16),
        grads=((count, width), B16),
        gains=((2, part), B16),
        all_gains=((n_shard, 2, part), B16),
        gain1=((1, width), F32),
        gain2=((1, width), F32),
        pk_qkv=((n_shard, part, 3 * part), B16),
        w_qkv=((width, 3 * part), B16),
        pk_in=((n_shard, part, 2 * hidden), B16),
        w_in=((width, 2 * hidden), B16),
        h1=((count, width), B16),
        heads=((3 * heads, count, HEAD_DIM), B16),
        probs=((heads, count, count), B16),
        att_heads=((heads, count, HEAD_DIM), B16),
        att=((count, part), B16),
        h2=((count, width), B16),
        act=((count, hidden), B16),
        gup=((count, 2 * hidden), B16),
        resid=((tok, width), F32),
        xhat1=((tok, width), F32),
        inv1=((tok, 1), F32),
        xhat2=((tok, width), F32),
        inv2=((tok, 1), F32),
        gres=((tok, width), F32),
        resid_b=((count, width), B16),
        gatt=((heads, count, HEAD_DIM), B16),
        gheads=((3 * heads, count, HEAD_DIM), F32),
        gproj=((count, 3 * part), B16),
        sums=((n_rep.bit_length() + 2, 16, LANES), F32),
        boxes=((n_rep.bit_length() + 1, 16, LANES), F32),
    )
    exchanges = ("att", "h2", "down", "h1")
    scratch.update(
        parts={name: ((count, width), B16) for name in exchanges},
        nears={name: ((2, tok, width), B16) for name in exchanges},
        outgoing={name: ((tok, width), B16) for name in exchanges},
        fars={name: ((tok, width), B16) for name in exchanges},
    )
    cfg.groups, cfg.padding, padded = [], [], {}
    for name, rows, swap, most in (
        ("down", hidden * width // LANES, False, 4),
        ("in", part * 2 * hidden // LANES, True, 7),
        ("out", part * width // LANES, False, 3),
        ("qkv", part * 3 * part // LANES, True, 7),
    ):
        streams, tall = streams_of(rows, n_rep, most)
        cfg.groups.append((name, streams, swap))
        if tall > rows:
            cfg.padding.append((name, rows))
        padded[name] = ((n_shard, tall, LANES) if swap else (tall, LANES), B16)
    scratch.update(acc=padded, box=padded)
    scratch.update({name: (value.shape, value.dtype) for name, value in ins.items()})
    plain = list(outs)
    outs.update(padded)

    def is_entry(item):
        return isinstance(item, tuple)

    spaces = jax.tree.map(lambda entry: pltpu.VMEM(*entry), scratch, is_leaf=is_entry)
    spaces["sems"] = pltpu.SemaphoreType.DMA((SEMAPHORES,))
    spaces, cfg.tree = jax.tree.flatten(spaces)
    cfg.inputs, cfg.names, cfg.sums = list(ins), plain, list(padded)
    middle = pl.pallas_call(
        functools.partial(layer_kernel, cfg),
        out_shape=tuple(jax.ShapeDtypeStruct(*entry) for entry in outs.values()),
        in_specs=[pl.BlockSpec(memory_space=pltpu.HBM)] * len(ins),
        out_specs=tuple([VMEM] * len(outs)),
        scratch_shapes=spaces,
        compiler_params=pltpu.CompilerParams(
            collective_id=0, has_side_effects=True, vmem_limit_bytes=cfg.limit
        ),
    )(*[pltpu.with_memory_space_constraint(value, pltpu.HBM) for value in ins.values()])
    anywhere = pl.BlockSpec(memory_space=pl.ANY)
    results = pl.pallas_call(
        functools.partial(finish_kernel, cfg),
        out_shape=tuple(jax.ShapeDtypeStruct(*entry) for entry in results.values()),
        in_specs=[VMEM] * len(middle),
        out_specs=tuple(VMEM if "gain" in name else anywhere for name in results),
        scratch_shapes=[
            pltpu.VMEM(*results[name]) for name in ("o_qkv", "o_out", "o_in", "o_down")
        ]
        + [pltpu.SemaphoreType.DMA((16,))],
        compiler_params=pltpu.CompilerParams(vmem_limit_bytes=cfg.finish_limit),
    )(*middle)
    output, grad_tokens, gain1, grad_qkv, grad_out, gain2, grad_in, grad_down = results
    return (
        output.reshape(1, tok, width),
        grad_tokens.reshape(1, tok, width),
        gain1.reshape(part),
        grad_qkv,
        grad_out,
        gain2.reshape(part),
        grad_in,
        grad_down,
    )


def solution(mesh):
    in_specs = (
        P("rep", "shard", None),
        P("shard"),
        P("shard", None),
        P("shard", None),
        P("shard"),
        P("shard", None),
        P("shard", None),
        P("rep", "shard", None),
    )
    out_specs = (
        P("rep", "shard", None),
        P("rep", "shard", None),
        P("shard"),
        P("shard", None),
        P("shard", None),
        P("shard"),
        P("shard", None),
        P("shard", None),
    )
    body = functools.partial(local, mesh.shape["shard"], mesh.shape["rep"])
    return jax.shard_map(body, mesh=mesh, in_specs=in_specs, out_specs=out_specs, check_vma=False)
```

```python
import functools
import heapq

import jax
import jax.numpy as jnp
import numpy as np
from jax import lax
from jax.experimental import pallas as pl
from jax.experimental.pallas import tpu as pltpu
from jax.sharding import PartitionSpec as P

HEAD_DIM = 64
EPSILON = 1e-05
THETA = 160000.0
SQRT_HALF = 0.7071067811865476
INV_SQRT_TAU = 0.3989422804014327
MESH_ID = pl.DeviceIdType.MESH
LANES = 128
VMEM = pl.BlockSpec(memory_space=pltpu.VMEM)
F32 = jnp.float32
B16 = jnp.bfloat16
SEMAPHORES = 640
HOP_US = 1.9
LINK_BYTES_PER_US = 90000.0


def normalize(values):
    mean_row = jnp.mean(values, axis=-1, keepdims=True)
    centred = values - mean_row
    variance = jnp.mean(centred * centred, axis=-1, keepdims=True)
    inverse = lax.rsqrt(variance + EPSILON)
    return (centred * inverse, inverse)


def norm_backward(grad_out, normed, inverse, gain):
    grad_normed = grad_out * gain
    gain_grad = jnp.sum(grad_out * normed, axis=0, keepdims=True)
    first = jnp.mean(grad_normed, axis=-1, keepdims=True)
    second = jnp.mean(grad_normed * normed, axis=-1, keepdims=True)
    return (inverse * (grad_normed - first - normed * second), gain_grad)


def gelu_pair(inner):
    cdf = 0.5 * (1.0 + lax.erf(inner * SQRT_HALF))
    return (inner * cdf, cdf + inner * jnp.exp(-0.5 * inner * inner) * INV_SQRT_TAU)


def dot(left, right):
    return jnp.dot(left, right, preferred_element_type=F32)


def outer_sum(left, right):
    return lax.dot_general(left, right, (((0,), (0,)), ((), ())), preferred_element_type=F32)


def times_transposed(left, right):
    return lax.dot_general(left, right, (((1,), (1,)), ((), ())), preferred_element_type=F32)


def flip(index, bit):
    return index + bit * (1 - 2 * ((index // bit) % 2))


def aligned(start, size, unit=16):
    if not isinstance(start, int):
        start = pl.multiple_of(start, unit)
    return pl.ds(start, size)


def remote(src, dst, sems, axis, target):
    return pltpu.make_async_remote_copy(
        src_ref=src,
        dst_ref=dst,
        send_sem=sems(),
        recv_sem=sems(),
        device_id={axis: target},
        device_id_type=MESH_ID,
    )


class Pool:
    def __init__(self, ref):
        self.ref, self.used = ref, 0

    def __call__(self):
        self.used += 1
        assert self.used <= SEMAPHORES
        return self.ref.at[self.used - 1]


class Place:
    def __init__(self):
        self.me = lax.axis_index("shard")
        self.rep = lax.axis_index("rep")
        self.core = flip(self.me, 1)
        self.chip = flip(self.me, 2)
        self.diagonal = flip(self.core, 2)


class AllGather:
    def __init__(self, place, sems, src, dst, tok, chunks):
        self.far, self.near, self.relays = [], [], []
        self.place, self.sems, self.dst, self.tok, self.chunks = place, sems, dst, tok, chunks
        size = tok // chunks
        for c in range(chunks):
            part = src.at[pl.ds(c * size, size)]
            self.far.append(remote(part, self.rows(place.me, c), sems, "shard", place.chip))
        for c in range(chunks):
            part = src.at[pl.ds(c * size, size)]
            self.near.append(remote(part, self.rows(place.me, c), sems, "shard", place.core))

    def rows(self, block, c):
        size = self.tok // self.chunks
        return self.dst.at[aligned(block * self.tok + c * size, size)]

    def start_far(self):
        for copy in self.far:
            copy.start()

    def start_near(self):
        for copy in self.near:
            copy.start()

    def relay(self, c):
        self.far[c].wait_recv()
        region = self.rows(self.place.chip, c)
        copy = remote(region, region, self.sems, "shard", self.place.core)
        copy.start()
        self.relays.append(copy)

    def relay_all(self):
        for c in range(self.chunks):
            self.relay(c)

    def finish_near(self):
        for copy in self.near:
            copy.wait_recv()

    def finish_far(self):
        for copy in self.relays:
            copy.wait_recv()

    def close(self):
        for copy in self.far + self.near + self.relays:
            copy.wait_send()


class ReduceScatter:
    def __init__(self, place, sems, part, near, outgoing, far, tok, chunks):
        self.place, self.sems, self.part, self.near = place, sems, part, near
        self.outgoing, self.far, self.tok, self.chunks = outgoing, far, tok, chunks
        self.size = tok // chunks
        self.first, self.second, self.third = [], [], []

    def rows(self, block, c):
        return aligned(block * self.tok + c * self.size, self.size)

    def piece(self, c):
        return pl.ds(c * self.size, self.size)

    def start(self, block, slot, copies):
        for c in range(self.chunks):
            copy = remote(
                self.part.at[self.rows(block, c)],
                self.near.at[slot, self.piece(c)],
                self.sems,
                "shard",
                self.place.core,
            )
            copy.start()
            copies.append(copy)

    def start_far(self):
        self.start(self.place.diagonal, 0, self.first)

    def start_near(self):
        self.start(self.place.core, 1, self.second)

    def forward(self):
        for c in range(self.chunks):
            self.first[c].wait_recv()
            piece = self.piece(c)
            mine = self.part[self.rows(self.place.chip, c)].astype(F32)
            self.outgoing[piece] = (mine + self.near[0, piece].astype(F32)).astype(B16)
            copy = remote(
                self.outgoing.at[piece], self.far.at[piece], self.sems, "shard", self.place.chip
            )
            copy.start()
            self.third.append(copy)

    def result(self):
        for copy in self.second + self.third:
            copy.wait_recv()
        mine = self.part[aligned(self.place.me * self.tok, self.tok)].astype(F32)
        return mine + self.near[1].astype(F32) + self.far[...].astype(F32)

    def close(self):
        for copy in self.first + self.second + self.third:
            copy.wait_send()


class Swap:
    def __init__(self, place, sems, source, packed, dest, kinds, relays):
        self.place, self.sems, self.source = place, sems, source
        self.packed, self.dest, self.kinds, self.relays = packed, dest, kinds, relays
        self.tall = source.shape[0]
        self.share = self.tall >> relays
        columns = dest.shape[1]
        cut = columns // LANES // 2 * LANES
        low = tuple(1 << i for i in range(relays))
        self.parts = []
        for first, size, order in ((0, cut, low), (cut, columns - cut, low[::-1])):
            position = 0
            for level, bit in enumerate(order):
                position = position + ((place.rep // bit) % 2) * (1 << level)
            self.parts.append((pl.ds(first, size), order, position))
        self.shared, self.whole = [], []

    def pack(self):
        blocks, _, columns = self.packed.shape
        size = columns // self.kinds
        for j in range(blocks):
            for kind in range(self.kinds):
                start = (kind * blocks + j) * size
                self.packed[j, :, kind * size : (kind + 1) * size] = self.source[
                    :, start : start + size
                ]

    def start_far(self):
        place = self.place
        for columns, order, position in self.parts:
            first = position * self.share
            for target in (place.chip, place.diagonal):
                copy = remote(
                    self.packed.at[target, aligned(first, self.share), columns],
                    self.dest.at[aligned(place.me * self.tall + first, self.share), columns],
                    self.sems,
                    "shard",
                    target,
                )
                copy.start()
                self.shared.append((target, columns, order, position, [copy]))

    def start_near(self):
        place = self.place
        mine = aligned(place.me * self.tall, self.tall)
        copy = remote(
            self.packed.at[place.core], self.dest.at[mine], self.sems, "shard", place.core
        )
        copy.start()
        self.whole.append(copy)
        self.dest[mine] = self.packed[place.me]

    def relay(self, level):
        if level >= self.relays:
            return
        for target, columns, order, position, copies in self.shared:
            copies[-1].wait_recv()
            length = self.share << level
            first = (position // (1 << level)) * length
            region = self.dest.at[aligned(target * self.tall + first, length), columns]
            copy = remote(region, region, self.sems, "rep", flip(self.place.rep, order[level]))
            copy.start()
            copies.append(copy)

    def finish(self):
        for entry in self.shared:
            entry[-1][-1].wait_recv()
        for copy in self.whole:
            copy.wait_recv()

    def close(self):
        for copy in self.whole:
            copy.wait_send()
        for entry in self.shared:
            for copy in entry[-1]:
                copy.wait_send()


def halves(order, index):
    length = 1 << len(order)
    offset = 0
    plan = []
    for bit in order:
        length //= 2
        side = (index // bit) % 2
        plan.append((bit, offset + side * length, offset + (1 - side) * length, length))
        offset = offset + side * length
    return plan


def streams_of(rows, n_rep, pattern):
    tiles = -(-rows // (16 * n_rep))
    low = tuple(1 << i for i in range(n_rep.bit_length() - 1))
    orders = {"A": low, "B": low[1::-1] + low[2:], "E": low[:1] + low[2:] + low[1:2]}
    most = min(len(pattern), tiles)
    streams = []
    base = 0
    for i in range(most):
        share = tiles // most + (i < tiles % most)
        streams.append((base, 16 * share, orders[pattern[i]]))
        base += 16 * share * n_rep
    return streams, base


class Schedule:
    def __init__(self):
        self.free = {}
        self.queue = []
        self.count = 0

    def put(self, item, now):
        for link, time in item.cost():
            start = max(now, self.free.get(link, 0.0))
            self.free[link] = start + time
        self.count += 1
        heapq.heappush(self.queue, (start + time + HOP_US, self.count, item))

    def launch(self, items, now):
        for item in items:
            item.begin()
            self.put(item, now)

    def pump(self, now, until=None):
        until = now if until is None else until
        while self.queue and self.queue[0][0] <= until:
            arrival, _, item = heapq.heappop(self.queue)
            item.advance()
            if not item.done():
                self.put(item, max(arrival, now))


class RepSum:
    def __init__(self, place, sems, stream, swap, acc, box, res):
        self.place, self.sems, self.swap = place, sems, swap
        self.base, self.rows, order = stream
        self.acc, self.box, self.res = acc, box, res
        self.steps = len(order)
        self.plan = halves(order, place.rep)
        self.started = []
        self.round = 0

    def at(self, ref, piece, length, lead=None):
        span = aligned(self.base + piece * self.rows, length * self.rows)
        if not self.swap:
            return ref.at[span]
        return ref.at[slice(None) if lead is None else lead, span]

    def begin(self):
        k, plan, steps, place, sems = self.round, self.plan, self.steps, self.place, self.sems
        acc, box, res = self.acc, self.box, self.res
        if k < steps:
            bit, _, sent, length = plan[k]
            source, target = self.at(acc, sent, length), self.at(box, length, length)
            copies = [remote(source, target, sems, "rep", flip(place.rep, bit))]
        elif k == steps:
            mine = plan[-1][1]
            if not self.swap:
                copies = [
                    pltpu.make_async_copy(self.at(acc, mine, 1), self.at(res, mine, 1), sems())
                ]
            else:
                target_block = self.at(res, mine, 1, place.me)
                copies = [
                    remote(self.at(acc, mine, 1, target), target_block, sems, "shard", target)
                    for target in (place.core, place.chip, place.diagonal)
                ]
                copies.append(
                    pltpu.make_async_copy(self.at(acc, mine, 1, place.me), target_block, sems())
                )
        else:
            bit, kept, _, length = plan[2 * steps - k]
            region = self.at(res, kept, length)
            copies = [remote(region, region, sems, "rep", flip(place.rep, bit))]
        for copy in copies:
            copy.start()
        self.started.append(copies)

    def finish(self):
        k = self.round
        copies = self.started[k]
        if k == self.steps:
            for copy in copies:
                copy.wait()
            return
        copies[0].wait_recv()
        if k > self.steps:
            return
        acc, box, base, rows = self.acc, self.box, self.base, self.rows
        _, kept, _, length = self.plan[k]
        blocks = range(acc.shape[0]) if self.swap else (None,)

        @pl.loop(0, length)
        def _(p):
            to = aligned(base + (kept + p) * rows, rows)
            of = aligned(base + (length + p) * rows, rows)
            for block in blocks:
                x, y = ((to,), (of,)) if block is None else ((block, to), (block, of))
                acc[x] = (acc[x].astype(F32) + box[y].astype(F32)).astype(B16)

    def advance(self):
        self.finish()
        self.round += 1
        if not self.done():
            self.begin()

    def done(self):
        return self.round > 2 * self.steps

    def cost(self):
        k, steps = self.round, self.steps
        blocks = self.acc.shape[0] if self.swap else 1
        piece = 2 * self.rows * LANES * 2 * blocks / LINK_BYTES_PER_US
        if k == steps:
            return [(-1, piece / 2 if self.swap else 0.0)]
        bit, _, _, length = self.plan[k if k < steps else 2 * steps - k]
        if bit > 2:
            return [(2, piece * length), (bit, 2 * piece * length)]
        return [(bit, piece * length)]

    def close(self):
        for k in range(2 * self.steps + 1):
            if k != self.steps:
                self.started[k][0].wait_send()


class Total:
    def __init__(self, place, sems, sums, boxes, bits):
        self.place, self.sems, self.sums, self.boxes, self.bits = place, sems, sums, boxes, bits
        self.copies = []
        self.round = 0

    def begin(self):
        level = len(self.copies)
        axis, bit = self.bits[level]
        index = self.place.me if axis == "shard" else self.place.rep
        copy = remote(
            self.sums.at[level], self.boxes.at[level], self.sems, axis, flip(index, bit)
        )
        copy.start()
        self.copies.append(copy)

    def advance(self):
        level = len(self.copies) - 1
        if level >= len(self.bits):
            return
        self.copies[level].wait_recv()
        self.sums[level + 1] = self.sums[level] + self.boxes[level]
        if level + 1 < len(self.bits):
            self.begin()
        else:
            self.copies.append(None)

    def done(self):
        return len(self.copies) > len(self.bits)

    def cost(self):
        return [(0, 0.0)]

    def close(self):
        for copy in self.copies[:-1]:
            copy.wait_send()


def pack_block(values, target, t):
    rows, columns = values.shape
    full, rest = divmod(columns, LANES)
    values = values.astype(B16)
    for j in range(full):
        target[t, j * rows : (j + 1) * rows] = values[:, j * LANES : (j + 1) * LANES]
    if rest:
        half = rows // 2
        tail = values[:, full * LANES :]
        target[t, full * rows : full * rows + half] = jnp.concatenate(
            [tail[:half], tail[half:]], axis=1
        )


def unpack_block(source, out, t, kinds):
    blocks = source.shape[0]
    rows, width = out.shape
    columns = width // blocks
    size = columns // kinds
    full, rest = divmod(columns, LANES)
    parts = [source[t, j * rows : (j + 1) * rows] for j in range(full)]
    if rest:
        tail = source[t, full * rows : full * rows + rows // 2]
        parts.append(jnp.concatenate([tail[:, :rest], tail[:, rest:]], axis=0))
    block = jnp.concatenate(parts, axis=1).astype(F32)
    for kind in range(kinds):
        start = (kind * blocks + t) * size
        out[:, start : start + size] = block[:, kind * size : (kind + 1) * size]


def pack_rows(values, target):
    rows = values.shape[0]
    values = values.astype(B16)
    for j in range(values.shape[1] // LANES):
        target[j * rows : (j + 1) * rows] = values[:, j * LANES : (j + 1) * LANES]


def unpack_rows(source, out):
    rows = out.shape[0]
    for j in range(out.shape[1] // LANES):
        out[:, j * LANES : (j + 1) * LANES] = source[j * rows : (j + 1) * rows].astype(F32)


def turned(values):
    lane = lax.broadcasted_iota(jnp.int32, values.shape, 1)
    half = HEAD_DIM // 2
    ahead = pltpu.roll(values, LANES - half, 1)
    behind = pltpu.roll(values, half, 1)
    return jnp.where(lane % HEAD_DIM < half, ahead, behind)


def query_scale(tile, part, rows):
    lane = lax.broadcasted_iota(jnp.int32, (rows, LANES), 1) + tile * LANES
    return jnp.where(lane < part, HEAD_DIM ** (-0.5), 1.0)


class Config:
    pass


def layer_kernel(cfg, *refs):
    r = Config()
    arguments = dict(zip(cfg.inputs, refs))
    refs = refs[len(cfg.inputs) :]
    r.__dict__.update(zip(cfg.names, refs))
    refs = refs[len(cfg.names) :]
    r.res = dict(zip(cfg.sums, refs))
    r.__dict__.update(jax.tree.unflatten(cfg.tree, refs[len(cfg.sums) :]))
    tok, width, part, heads, hidden = cfg.tok, cfg.width, cfg.part, cfg.heads, cfg.hidden
    n_shard, count, chunks = cfg.n_shard, cfg.count, cfg.chunks
    place = Place()
    sems = Pool(r.sems)
    me, core, chip, diagonal = place.me, place.core, place.chip, place.diagonal
    rep_bits = [1 << b for b in range(cfg.n_rep.bit_length() - 1)]
    partners = [("shard", core), ("shard", chip), ("shard", diagonal)]
    partners += [("rep", flip(place.rep, bit)) for bit in rep_bits]
    barrier = pltpu.get_barrier_semaphore()
    for axis, target in partners:
        pl.semaphore_signal(barrier, inc=1, device_id={axis: target}, device_id_type=MESH_ID)
    loads = {}
    for name in cfg.inputs:
        loads[name] = pltpu.make_async_copy(arguments[name], getattr(r, name), sems())
        loads[name].start()
    own = aligned(me * tok, tok)
    half = count // 2
    near_start = (me // 2) * half
    far_start = (chip // 2) * half

    qkv = Swap(place, sems, r.qkv, r.pk_qkv, r.w_qkv, 3, cfg.relays)
    win = Swap(place, sems, r.win, r.pk_in, r.w_in, 2, cfg.relays)
    tokens = AllGather(place, sems, r.tokens, r.toks, tok, chunks)
    grads = AllGather(place, sems, r.grad, r.grads, tok, 2)
    gains = [
        remote(r.gains, r.all_gains.at[me], sems, "shard", target)
        for target in (core, chip, diagonal)
    ]
    loads["gain_one"].wait()
    loads["gain_two"].wait()
    r.gains[0:1] = r.gain_one[...].reshape(1, part)
    r.gains[1:2] = r.gain_two[...].reshape(1, part)
    loads["qkv"].wait()
    qkv.pack()
    for name in ("tokens", "win", "grad"):
        loads[name].wait()
    pl.semaphore_wait(barrier, len(partners))
    for copy in gains:
        copy.start()
    qkv.start_far()
    tokens.start_far()
    tokens.start_near()
    qkv.start_near()
    r.toks[own] = r.tokens[...]
    r.grads[own] = r.grad[...]
    r.all_gains[me] = r.gains[...]
    win.pack()
    for name, rows in cfg.padding:
        acc = r.acc[name]
        if len(acc.shape) == 3:
            acc[:, rows:] = jnp.zeros((n_shard, acc.shape[1] - rows, LANES), B16)
        else:
            acc[rows:] = jnp.zeros((acc.shape[0] - rows, LANES), B16)
    normed, inverse = normalize(r.tokens[...].astype(F32))
    r.xhat1[...] = normed
    r.inv1[...] = inverse
    r.sums[0] = jnp.zeros((16, LANES), F32)
    for copy in gains:
        copy.wait_recv()
    for t in range(n_shard):
        columns = slice(t * part, (t + 1) * part)
        r.gain1[:, columns] = r.all_gains[t, 0:1].astype(F32)
        r.gain2[:, columns] = r.all_gains[t, 1:2].astype(F32)

    def normalize_half(start):
        @pl.loop(0, half // tok)
        def _(i):
            rows = aligned(start + i * tok, tok)
            values, _ = normalize(r.toks[rows].astype(F32))
            r.h1[rows] = (values * r.gain1[...]).astype(B16)

    tokens.finish_near()
    normalize_half(near_start)
    qkv.relay(0)
    win.start_far()
    grads.start_far()
    grads.start_near()
    win.start_near()
    qkv.relay(1)
    tokens.relay_all()
    tokens.finish_far()
    normalize_half(far_start)
    qkv.finish()

    loads["cosine"].wait()
    loads["sine"].wait()
    @pl.loop(0, 2)
    def _(i):
        rows = aligned(i * half, half)
        projected = dot(r.h1[rows], r.w_qkv[...])
        cosine, sine = r.cosine[rows], r.sine[rows]
        for j in range(3 * part // LANES + 1):
            size = min(LANES, 3 * part - j * LANES)
            tile = projected[:, j * LANES : j * LANES + size]
            if (j + 1) * LANES <= 2 * part:
                tile = tile * cosine + turned(tile) * sine
                if j * LANES < part:
                    tile = tile * query_scale(j, part, half)
            tile = tile.astype(B16)
            for k in range(size // HEAD_DIM):
                index = j * (LANES // HEAD_DIM) + k
                r.heads[index, rows] = tile[:, k * HEAD_DIM : (k + 1) * HEAD_DIM]

    @pl.loop(0, heads)
    def _(h):
        key, value = r.heads[heads + h], r.heads[2 * heads + h]
        for b in range(2):
            rows = pl.ds(b * half, half)
            scores = times_transposed(r.heads[h, rows], key)
            maxima = jnp.max(scores, axis=-1, keepdims=True)
            expo = jnp.exp(scores - maxima)
            total = jnp.sum(expo, axis=-1, keepdims=True)
            probs = (expo * (1.0 / total)).astype(B16)
            r.probs[h, rows] = probs
            r.att_heads[h, rows] = dot(probs, value).astype(B16)

    win.relay(0)
    for h in range(heads):
        r.att[:, h * HEAD_DIM : (h + 1) * HEAD_DIM] = r.att_heads[h]

    def reduce(name, chunks=chunks):
        return ReduceScatter(
            place, sems, r.parts[name], r.nears[name], r.outgoing[name], r.fars[name], tok, chunks
        )

    def project(start):
        rows = aligned(start, half)
        r.parts["att"][rows] = dot(r.att[rows], r.w_out[...]).astype(B16)

    mixed = reduce("att")
    loads["w_out"].wait()
    loads["down"].wait()
    project(far_start)
    mixed.start_far()
    project(near_start)
    mixed.start_near()
    mixed.forward()
    win.relay(1)
    grads.relay_all()
    resid = r.tokens[...].astype(F32) + mixed.result()
    r.resid[...] = resid
    normed, inverse = normalize(resid)
    r.xhat2[...] = normed
    r.inv2[...] = inverse
    scaled = (normed * r.gain2[...]).astype(B16)
    r.h2[own] = scaled
    second = AllGather(place, sems, r.h2.at[own], r.h2, tok, chunks)
    second.start_far()
    second.start_near()
    win.finish()
    grads.finish_near()
    grads.finish_far()

    def feed_forward(start):
        rows = aligned(start, half)
        upper = dot(r.h2[rows], r.w_in[...])
        inner, gate = upper[:, :hidden], upper[:, hidden:]
        value, slope = gelu_pair(inner)
        act = (value * gate).astype(B16)
        r.act[rows] = act
        grad_act = times_transposed(r.grads[rows], r.down[...])
        grad_upper = jnp.concatenate(
            [grad_act * gate * slope, grad_act * value], axis=-1
        ).astype(B16)
        r.gup[rows] = grad_upper
        r.parts["h2"][rows] = times_transposed(grad_upper, r.w_in[...]).astype(B16)
        r.parts["down"][rows] = dot(act, r.down[...]).astype(B16)

    back2, down = reduce("h2"), reduce("down", 2)
    second.finish_near()
    feed_forward(near_start)
    back2.start_near()
    second.relay_all()
    second.finish_far()
    feed_forward(far_start)
    back2.start_far()
    down.start_near()
    down.start_far()

    groups = {}
    for name, streams, swap in cfg.groups:
        groups[name] = [
            RepSum(place, sems, stream, swap, r.acc[name], r.box[name], r.res[name])
            for stream in streams
        ]
    plan = Schedule()

    pack_rows(outer_sum(r.act[...], r.grads[...]), r.acc["down"])
    plan.launch(groups["down"], 0.0)
    back2.forward()

    def pack_pairs(left, right, target):
        for i in range(n_shard // 2):
            columns = slice(i * 2 * part, (i + 1) * 2 * part)
            values = outer_sum(left[:, columns], right[...])
            pack_block(values[:part], target, 2 * i)
            pack_block(values[part:], target, 2 * i + 1)

    pack_pairs(r.h2, r.gup, r.acc["in"])
    plan.launch(groups["in"], 1.6)
    plan.pump(1.6, 5.6)
    grad_h2 = back2.result()
    back, gain_grad = norm_backward(grad_h2, r.xhat2[...], r.inv2[...], r.gain2[...])
    for j in range(width // LANES):
        r.sums[0, 8 + j : 9 + j] = gain_grad[:, j * LANES : (j + 1) * LANES]
    grad_resid = r.grad[...].astype(F32) + back
    r.gres[...] = grad_resid
    r.resid_b[own] = grad_resid.astype(B16)
    third = AllGather(place, sems, r.resid_b.at[own], r.resid_b, tok, chunks)
    third.start_far()
    third.start_near()
    down.forward()
    plan.pump(7.0)

    def attention_grad(start):
        rows = aligned(start, half)
        values = times_transposed(r.resid_b[rows], r.w_out[...]).astype(B16)
        for h in range(heads):
            r.gatt[h, rows] = values[:, h * HEAD_DIM : (h + 1) * HEAD_DIM]

    third.finish_near()
    attention_grad(near_start)
    plan.pump(8.5)
    for c in range(chunks):
        third.relay(c)
        plan.pump(12.5 - 3.6 * (chunks - 1 - c) / chunks)
    plan.pump(12.0)
    third.finish_far()
    attention_grad(far_start)
    pack_rows(outer_sum(r.att[...], r.resid_b[...]), r.acc["out"])
    plan.pump(13.5)
    plan.launch(groups["out"], 13.5)

    for h in range(heads):
        key, value, query = r.heads[heads + h], r.heads[2 * heads + h], r.heads[h]
        grad_value = jnp.zeros((count, HEAD_DIM), F32)
        grad_key = jnp.zeros((count, HEAD_DIM), F32)
        for b in range(2):
            rows = pl.ds(b * half, half)
            grad_head = r.gatt[h, rows]
            probs = r.probs[h, rows]
            attended = r.att_heads[h, rows].astype(F32)
            delta = jnp.sum(grad_head.astype(F32) * attended, axis=-1, keepdims=True)
            grad_value = grad_value + outer_sum(probs, grad_head)
            grad_probs = times_transposed(grad_head, value)
            grad_scores = (probs.astype(F32) * (grad_probs - delta)).astype(B16)
            r.gheads[h, rows] = dot(grad_scores, key)
            grad_key = grad_key + outer_sum(grad_scores, query[b * half : (b + 1) * half])
        r.gheads[heads + h] = grad_key
        r.gheads[2 * heads + h] = grad_value
        plan.pump(14.4 + 0.9 * h)

    grad_parts = reduce("h1")

    def project_back(start):
        rows = aligned(start, half)
        cosine, sine = r.cosine[rows], r.sine[rows]
        for j in range(3 * part // LANES + 1):
            size = min(LANES, 3 * part - j * LANES)
            index = j * (LANES // HEAD_DIM)
            tile = jnp.concatenate(
                [r.gheads[index + k, rows] for k in range(size // HEAD_DIM)], axis=-1
            )
            if (j + 1) * LANES <= 2 * part:
                tile = tile * cosine - turned(tile) * sine
                if j * LANES < part:
                    tile = tile * query_scale(j, part, half)
            r.gproj[rows, j * LANES : j * LANES + size] = tile.astype(B16)
        r.parts["h1"][rows] = times_transposed(r.gproj[rows], r.w_qkv[...]).astype(B16)

    project_back(far_start)
    grad_parts.start_far()
    project_back(near_start)
    grad_parts.start_near()
    plan.pump(17.9)
    pack_pairs(r.h1, r.gproj, r.acc["qkv"])
    plan.launch(groups["qkv"], 18.9)
    grad_parts.forward()
    r.o_output[...] = (r.resid[...] + down.result()).astype(B16)
    plan.pump(19.5, 24.0)
    grad_h1 = grad_parts.result()
    back, gain_grad = norm_backward(grad_h1, r.xhat1[...], r.inv1[...], r.gain1[...])
    for j in range(width // LANES):
        r.sums[0, j : j + 1] = gain_grad[:, j * LANES : (j + 1) * LANES]
    small = Total(
        place, sems, r.sums, r.boxes,
        [("shard", 1), ("shard", 2)] + [("rep", bit) for bit in rep_bits],
    )
    plan.launch([small], 25.0)
    r.o_tokens[...] = r.gres[...] + back
    plan.pump(25.5, float("inf"))
    r.o_total[...] = r.sums[len(small.bits)]
    for copy in gains:
        copy.wait_send()
    for item in [qkv, win, tokens, grads, second, third, mixed, back2, down, grad_parts]:
        item.close()
    for item in sum(groups.values(), [small]):
        item.close()


def finish_kernel(cfg, *refs):
    ins, outs = refs[:7], refs[7:15]
    stage_qkv, stage_out, stage_in, stage_down, sems = refs[15:]
    output, grad_tokens, total, res_down, res_in, res_out, res_qkv = ins
    o_output, o_tokens, o_gain1, o_qkv, o_out, o_gain2, o_in, o_down = outs
    copies = []

    def send(source, target, pieces):
        size = source.shape[0] // pieces
        for i in range(pieces):
            rows = pl.ds(i * size, size)
            copy = pltpu.make_async_copy(source.at[rows], target.at[rows], sems.at[len(copies)])
            copy.start()
            copies.append(copy)

    send(output, o_output, 1)
    send(grad_tokens, o_tokens, 1)
    for t in range(cfg.n_shard):
        unpack_block(res_qkv, stage_qkv, t, 3)
    send(stage_qkv, o_qkv, 4)
    for t in range(cfg.n_shard):
        unpack_block(res_in, stage_in, t, 2)
    send(stage_in, o_in, 4)
    unpack_rows(res_down, stage_down)
    send(stage_down, o_down, 2)
    unpack_rows(res_out, stage_out)
    send(stage_out, o_out, 2)
    me = lax.axis_index("shard")
    for out, at in ((o_gain1, 0), (o_gain2, 8)):
        row = jnp.concatenate(
            [total[at + j : at + j + 1] for j in range(cfg.width // LANES)], axis=1
        )
        picked = jnp.zeros((1, cfg.part), F32)
        for t in range(cfg.n_shard):
            picked = jnp.where(me == t, row[:, t * cfg.part : (t + 1) * cfg.part], picked)
        out[...] = picked
    for copy in copies:
        copy.wait()


def rotary_tables(count):
    half = HEAD_DIM // 2
    freq = THETA ** (-np.arange(half, dtype=np.float64) * 2.0 / HEAD_DIM)
    angles = np.arange(count, dtype=np.float64)[:, None] * freq[None, :]
    angles = np.concatenate([angles, angles], axis=-1)
    sign = np.where(np.arange(HEAD_DIM) < half, -1.0, 1.0)
    repeat = LANES // HEAD_DIM
    cosine = np.tile(np.cos(angles), (1, repeat))
    sine = np.tile(np.sin(angles) * sign, (1, repeat))
    return cosine.astype(np.float32), sine.astype(np.float32)


def local(
    n_shard, n_rep, tokens, gain_one, qkv_weight, out_weight, gain_two, in_weight, down_weight,
    grad_output
):
    tok, width = tokens.shape[1:]
    cfg = Config()
    cfg.n_shard, cfg.n_rep, cfg.tok, cfg.width = n_shard, n_rep, tok, width
    cfg.part = part = width // n_shard
    cfg.heads = heads = part // HEAD_DIM
    cfg.hidden = hidden = down_weight.shape[0]
    cfg.count = count = tok * n_shard
    cfg.chunks = 4
    cfg.limit = 44 * 1024 * 1024
    cfg.finish_limit = 16 * 1024 * 1024
    cfg.relays = min(2, n_rep.bit_length() - 1)
    while cfg.relays and part % (16 << cfg.relays):
        cfg.relays -= 1
    cosine, sine = rotary_tables(count)
    ins = dict(
        gain_one=gain_one,
        gain_two=gain_two,
        qkv=qkv_weight,
        tokens=tokens.reshape(tok, width),
        win=in_weight,
        grad=grad_output.reshape(tok, width),
        cosine=jnp.asarray(cosine),
        sine=jnp.asarray(sine),
        w_out=out_weight,
        down=down_weight,
    )
    outs = dict(
        o_output=((tok, width), B16),
        o_tokens=((tok, width), F32),
        o_total=((16, LANES), F32),
    )
    results = dict(
        o_output=((tok, width), B16),
        o_tokens=((tok, width), F32),
        o_gain1=((1, part), F32),
        o_qkv=((part, 3 * width), F32),
        o_out=((part, width), F32),
        o_gain2=((1, part), F32),
        o_in=((part, 2 * hidden * n_shard), F32),
        o_down=((hidden, width), F32),
    )
    scratch = dict(
        toks=((count, width), B16),
        grads=((count, width), B16),
        gains=((2, part), B16),
        all_gains=((n_shard, 2, part), B16),
        gain1=((1, width), F32),
        gain2=((1, width), F32),
        pk_qkv=((n_shard, part, 3 * part), B16),
        w_qkv=((width, 3 * part), B16),
        pk_in=((n_shard, part, 2 * hidden), B16),
        w_in=((width, 2 * hidden), B16),
        h1=((count, width), B16),
        heads=((3 * heads, count, HEAD_DIM), B16),
        probs=((heads, count, count), B16),
        att_heads=((heads, count, HEAD_DIM), B16),
        att=((count, part), B16),
        h2=((count, width), B16),
        act=((count, hidden), B16),
        gup=((count, 2 * hidden), B16),
        resid=((tok, width), F32),
        xhat1=((tok, width), F32),
        inv1=((tok, 1), F32),
        xhat2=((tok, width), F32),
        inv2=((tok, 1), F32),
        gres=((tok, width), F32),
        resid_b=((count, width), B16),
        gatt=((heads, count, HEAD_DIM), B16),
        gheads=((3 * heads, count, HEAD_DIM), F32),
        gproj=((count, 3 * part), B16),
        sums=((n_rep.bit_length() + 2, 16, LANES), F32),
        boxes=((n_rep.bit_length() + 1, 16, LANES), F32),
    )
    exchanges = ("att", "h2", "down", "h1")
    scratch.update(
        parts={name: ((count, width), B16) for name in exchanges},
        nears={name: ((2, tok, width), B16) for name in exchanges},
        outgoing={name: ((tok, width), B16) for name in exchanges},
        fars={name: ((tok, width), B16) for name in exchanges},
    )
    cfg.groups, cfg.padding, padded = [], [], {}
    for name, rows, swap, pattern in (
        ("down", hidden * width // LANES, False, "EBAA"),
        ("in", part * 2 * hidden // LANES, True, "ABAAAAA"),
        ("out", part * width // LANES, False, "AAE"),
        ("qkv", part * 3 * part // LANES, True, "AAAABAB"),
    ):
        streams, tall = streams_of(rows, n_rep, pattern)
        cfg.groups.append((name, streams, swap))
        if tall > rows:
            cfg.padding.append((name, rows))
        padded[name] = ((n_shard, tall, LANES) if swap else (tall, LANES), B16)
    scratch.update(acc=padded, box=padded)
    scratch.update({name: (value.shape, value.dtype) for name, value in ins.items()})
    plain = list(outs)
    outs.update(padded)

    def is_entry(item):
        return isinstance(item, tuple)

    spaces = jax.tree.map(lambda entry: pltpu.VMEM(*entry), scratch, is_leaf=is_entry)
    spaces["sems"] = pltpu.SemaphoreType.DMA((SEMAPHORES,))
    spaces, cfg.tree = jax.tree.flatten(spaces)
    cfg.inputs, cfg.names, cfg.sums = list(ins), plain, list(padded)
    middle = pl.pallas_call(
        functools.partial(layer_kernel, cfg),
        out_shape=tuple(jax.ShapeDtypeStruct(*entry) for entry in outs.values()),
        in_specs=[pl.BlockSpec(memory_space=pltpu.HBM)] * len(ins),
        out_specs=tuple([VMEM] * len(outs)),
        scratch_shapes=spaces,
        compiler_params=pltpu.CompilerParams(
            collective_id=0, has_side_effects=True, vmem_limit_bytes=cfg.limit
        ),
    )(*[pltpu.with_memory_space_constraint(value, pltpu.HBM) for value in ins.values()])
    anywhere = pl.BlockSpec(memory_space=pl.ANY)
    results = pl.pallas_call(
        functools.partial(finish_kernel, cfg),
        out_shape=tuple(jax.ShapeDtypeStruct(*entry) for entry in results.values()),
        in_specs=[VMEM] * len(middle),
        out_specs=tuple(VMEM if "gain" in name else anywhere for name in results),
        scratch_shapes=[
            pltpu.VMEM(*results[name]) for name in ("o_qkv", "o_out", "o_in", "o_down")
        ]
        + [pltpu.SemaphoreType.DMA((16,))],
        compiler_params=pltpu.CompilerParams(vmem_limit_bytes=cfg.finish_limit),
    )(*middle)
    output, grad_tokens, gain1, grad_qkv, grad_out, gain2, grad_in, grad_down = results
    return (
        output.reshape(1, tok, width),
        grad_tokens.reshape(1, tok, width),
        gain1.reshape(part),
        grad_qkv,
        grad_out,
        gain2.reshape(part),
        grad_in,
        grad_down,
    )


def solution(mesh):
    in_specs = (
        P("rep", "shard", None),
        P("shard"),
        P("shard", None),
        P("shard", None),
        P("shard"),
        P("shard", None),
        P("shard", None),
        P("rep", "shard", None),
    )
    out_specs = (
        P("rep", "shard", None),
        P("rep", "shard", None),
        P("shard"),
        P("shard", None),
        P("shard", None),
        P("shard"),
        P("shard", None),
        P("shard", None),
    )
    body = functools.partial(local, mesh.shape["shard"], mesh.shape["rep"])
    return jax.shard_map(body, mesh=mesh, in_specs=in_specs, out_specs=out_specs, check_vma=False)
```
